256 devices in a mesh: dom: 64 (over z, x, core), tp: 4 (over y).
Axes of the slice: x: 4, y: 4, z: 8, core: 2. Of those that a mesh axis runs over, the one named last changes fastest.
Arguments:
- state: bfloat16 [2, 65536, 512], P(None, 'dom'), may hold values from -6 to 6
- norm_gain: float32 [2, 2, 512], replicated, may hold values from 0.1 to 1.9
- norm_shift: float32 [2, 2, 512], replicated, may hold values from -3 to 3
- qkv_weight: bfloat16 [512, 3, 512], P(None, None, 'tp'), may hold values from -0.5 to 0.5
- out_weight: bfloat16 [512, 512], P('tp'), may hold values from -0.25 to 0.25
- up_weight: bfloat16 [512, 2048], P(None, 'tp'), may hold values from -0.25 to 0.25
- down_weight: bfloat16 [2048, 512], P('tp'), may hold values from -0.125 to 0.125
- neighbours: int32 [512, 8], P('dom'), may hold values from 0 to 511, as said below
- counts: int32 [512], P('dom'), may hold values from 2 to 8, as said below
Outputs:
- layer_out: bfloat16 [2, 65536, 512], P(None, 'dom', 'tp')
The draws below stay inside these ranges and needn't reach their ends.
Inputs may be any that keep to these rules, and one draw needn't show every extreme that they name: `neighbours`: entry 0 of row b is b itself; the other 7 entries are distinct blocks whose partition (block // 8) lies at most two partitions before or after b's on a closed chain of partitions, block numbers taken modulo 512. `counts`: every partition has a block whose count is 8.
All inputs are finite; a program needn't handle non-finite values.
Results may differ from the reference program's by a relative error of at most 0.017.
Values may be sent and summed in bfloat16 or wider, within the bound.
No kernel may reach another device: no remote copies, remote signals or barrier semaphores. Data moves between devices by JAX's collectives and lax.ppermute only.
A program may use at most 64 MiB of HBM per device.

```python
import math
import jax
import jax.numpy as jnp
from jax import lax

D = 512
HEADS = 4
FF = 2048
NODE_BLK = 128
KMAX = 8
S = 2
BLK_DEV = 8
BLOCKS = 512
NODES = 65536
N_TP = 4


def draw_neighbours(key, part):
    window = 5 * BLK_DEV
    row_keys = jax.random.split(key, BLOCKS)

    def one_row(row_key, block_id):
        chosen_slots = jax.random.permutation(row_key, window - 1)[:KMAX - 1]
        within = block_id % BLK_DEV
        self_slot = 2 * BLK_DEV + within
        offsets = chosen_slots + (chosen_slots >= self_slot).astype(jnp.int32)
        others = jnp.mod(block_id - within - 2 * BLK_DEV + offsets, BLOCKS)
        return jnp.concatenate([block_id[None], others]).astype(jnp.int32)
    return jax.vmap(one_row)(row_keys, jnp.arange(BLOCKS, dtype=jnp.int32))


def draw_counts(key, part):
    base_counts = jax.random.randint(key, (BLOCKS,), 2, KMAX + 1)
    full_slot = jax.random.randint(jax.random.fold_in(key, 7), (BLOCKS // BLK_DEV,), 0, BLK_DEV)
    within = jnp.arange(BLOCKS, dtype=jnp.int32) % BLK_DEV
    return jnp.where(within == jnp.repeat(full_slot, BLK_DEV), KMAX, base_counts).astype(jnp.int32)


def shard_levels(rng, extent, cuts, least, largest):
    def one(position, blocks):
        heights = jax.random.uniform(jax.random.fold_in(jax.random.fold_in(rng, 6), position), (blocks,), jnp.float32, least / len(cuts), largest / len(cuts))
        return jnp.repeat(jnp.exp(heights), extent[position] // blocks).reshape((-1,) + (1,) * (len(extent) - position - 1))

    factor_of = one(*cuts[0])
    for cut in cuts[1:]:
        factor_of = factor_of * one(*cut)
    return factor_of


def gaussian(rng, extent, deviation, reach, pieces=(), held_as=jnp.bfloat16):
    entries = jax.random.normal(rng, extent, jnp.float32) * deviation
    if len(pieces) > 0:
        entries = shard_levels(rng, extent, pieces, -0.22, 0.18) * entries
    return jnp.clip(entries, min=-reach, max=reach).astype(held_as)


def setup_inputs(seed: int = 0) -> dict:
    keys = jax.random.split(jax.random.key(seed), 10)
    return {
        "state": gaussian(keys[0], (S, NODES, D), 1.0, 6.0, ((1, 64),)),
        "norm_gain": jnp.clip(1.0 + 0.18 * jax.random.normal(keys[1], (2, S, D), jnp.float32), 0.1, 1.9),
        "norm_shift": gaussian(keys[2], (2, S, D), 0.5, 3.0, (), jnp.float32),
        "qkv_weight": gaussian(keys[3], (D, 3, D), (D // 4) ** -0.5, 0.5, ((2, 4),)),
        "out_weight": gaussian(keys[4], (D, D), D ** -0.5, 0.25, ((0, 4),)),
        "up_weight": gaussian(keys[5], (D, FF), D ** -0.5, 0.25, ((1, 4),)),
        "down_weight": gaussian(keys[6], (FF, D), FF ** -0.5, 0.125, ((0, 4),)),
        "neighbours": draw_neighbours(jax.random.fold_in(keys[9], 71), 0),
        "counts": draw_counts(jax.random.fold_in(keys[9], 71), 0),
    }


def layer_norm(values, gain_row, shift_row):
    row_mean = lax.optimization_barrier(jnp.mean(values, axis=-1, keepdims=True))
    centred = values - row_mean
    spread = lax.optimization_barrier(jnp.mean(centred * centred, axis=-1, keepdims=True))
    return centred * lax.rsqrt(spread + 1e-05) * gain_row + shift_row

def reference(state, norm_gain, norm_shift, qkv_weight, out_weight, up_weight, down_weight, neighbours, counts):
    samples, node_count, feat_width = state.shape
    block_count = node_count // NODE_BLK
    head_size = feat_width // HEADS
    head_cols = feat_width // N_TP
    unit_cols = FF // N_TP
    resid_in = state.astype(jnp.float32)
    normed = layer_norm(resid_in, norm_gain[0][:, None, :], norm_shift[0][:, None, :]).astype(jnp.bfloat16)
    projected = jnp.einsum('snd,dce->snce', normed.astype(jnp.float32), qkv_weight.astype(jnp.float32)).astype(jnp.bfloat16)
    projected = projected.reshape(samples, block_count, NODE_BLK, 3, HEADS, head_size)
    slot_ids = jnp.arange(KMAX * NODE_BLK, dtype=jnp.int32) // NODE_BLK

    def attend(block_idx):
        queries = projected[:, block_idx, :, 0].astype(jnp.float32)
        chosen = projected[:, neighbours[block_idx]]
        chosen = chosen.reshape(samples, KMAX * NODE_BLK, 3, HEADS, head_size).astype(jnp.float32)
        scores = jnp.einsum('sqhe,skhe->shqk', queries, chosen[:, :, 1]) / math.sqrt(head_size)
        live_mask = slot_ids < counts[block_idx]
        masked = jnp.where(live_mask, scores, -1e+30)
        row_top = lax.optimization_barrier(jnp.max(masked, axis=-1, keepdims=True))
        weights = jnp.exp(masked - row_top)
        weights = (weights / lax.optimization_barrier(jnp.sum(weights, axis=-1, keepdims=True))).astype(jnp.bfloat16)
        return jnp.einsum('shqk,skhe->sqhe', weights.astype(jnp.float32), chosen[:, :, 2]).astype(jnp.bfloat16)
    heads_out = lax.map(attend, jnp.arange(block_count, dtype=jnp.int32))
    heads_out = jnp.transpose(heads_out, (1, 0, 2, 3, 4)).reshape(samples * node_count, feat_width)
    attn_sum = jnp.zeros((samples * node_count, feat_width), jnp.float32)
    for tp_rank in range(N_TP):
        col_first = tp_rank * head_cols
        term_part = jnp.dot(heads_out[:, col_first:col_first + head_cols], out_weight[col_first:col_first + head_cols], preferred_element_type=jnp.float32).astype(jnp.bfloat16)
        term_part = lax.optimization_barrier(term_part)
        attn_sum = attn_sum + term_part.astype(jnp.float32)
    residual = resid_in.reshape(samples * node_count, feat_width) + attn_sum
    normed2 = layer_norm(residual.reshape(samples, node_count, feat_width), norm_gain[1][:, None, :], norm_shift[1][:, None, :]).astype(jnp.bfloat16)
    normed2 = normed2.reshape(samples * node_count, feat_width)
    hidden = jax.nn.silu(jnp.dot(normed2, up_weight, preferred_element_type=jnp.float32)).astype(jnp.bfloat16)
    update = jnp.zeros((samples * node_count, feat_width), jnp.float32)
    for tp_rank in range(N_TP):
        unit_first = tp_rank * unit_cols
        term_part = jnp.dot(hidden[:, unit_first:unit_first + unit_cols], down_weight[unit_first:unit_first + unit_cols], preferred_element_type=jnp.float32).astype(jnp.bfloat16)
        term_part = lax.optimization_barrier(term_part)
        update = update + term_part.astype(jnp.float32)
    return (residual + update).astype(jnp.bfloat16).reshape(samples, node_count, feat_width)
```

```python
import functools
import math

import jax
import jax.numpy as jnp
from jax import lax
from jax.experimental import pallas as pl
from jax.experimental.pallas import tpu as pltpu
from jax.sharding import PartitionSpec as P

HEADS = 4
NODE_BLK = 128
KMAX = 8
ROWS = 256
VMEM_LIMIT = 56 * 1024 * 1024


def bf(v):
    return v.astype(jnp.bfloat16)


def normalise(values, gain, shift):
    mean = jnp.mean(values, axis=-1, keepdims=True)
    centred = values - mean
    spread = jnp.mean(centred * centred, axis=-1, keepdims=True)
    return centred * lax.rsqrt(spread + 1e-05) * gain + shift


def matmul(a, b):
    return jnp.dot(a, b, preferred_element_type=jnp.float32)


def kv_kernel(x_ref, norm_ref, w0, w1, w2, w3a, w3b, *rest):
    kv_ref = rest[-1]
    normed = bf(normalise(x_ref[...].astype(jnp.float32), norm_ref[0:1], norm_ref[1:2]))
    cols = []
    for w in (w0, w1, w2):
        cols += [w[1], w[2]]
    for c in (1, 2):
        cols.append(jnp.concatenate([w3a[c], w3b[c]], axis=0))
    out = bf(matmul(normed, jnp.concatenate(cols, axis=1)))
    kv_ref[...] = out.reshape(kv_ref.shape)


def project_kv(x, norms, weights, kv, slot, per_dev, slots):
    rows, width = x.shape
    steps = rows // ROWS
    per_step = ROWS // NODE_BLK
    held = pl.BlockSpec(memory_space=pltpu.VMEM)
    specs = [pl.BlockSpec((ROWS, width), lambda i: (i, 0))] + [held] * (1 + len(weights))
    args = [x, norms, *weights]
    aliases = {}
    if kv is not None:
        specs.append(pl.BlockSpec(memory_space=pl.ANY))
        args.append(kv)
        aliases = {len(args) - 1: 0}
    kv_width = 2 * width
    return pl.pallas_call(
        kv_kernel,
        grid=(steps,),
        in_specs=specs,
        out_specs=pl.BlockSpec(
            (per_step, NODE_BLK, kv_width), lambda i: (slot * steps + i, 0, 0)
        ),
        out_shape=jax.ShapeDtypeStruct((slots * per_dev, NODE_BLK, kv_width), jnp.bfloat16),
        input_output_aliases=aliases,
        name="kv_rows",
        compiler_params=pltpu.CompilerParams(vmem_limit_bytes=24 * 1024 * 1024),
        cost_estimate=pl.CostEstimate(
            flops=2 * rows * width * kv_width, bytes_accessed=6 * rows * width, transcendentals=0
        ),
    )(*args)


def q_kernel(place_ref, x_ref, norm_ref, w0, w1, w2, w3a, w3b, q_ref):
    normed = bf(normalise(x_ref[0].astype(jnp.float32), norm_ref[0:1], norm_ref[1:2]))
    cols = [w0[0], w1[0], w2[0], jnp.concatenate([w3a[0], w3b[0]], axis=0)]
    q_ref[...] = bf(matmul(normed, jnp.concatenate(cols, axis=1)))


def project_q(place, state, norms, weights, rows):
    width = state.shape[2]
    held = pl.BlockSpec(memory_space=pltpu.VMEM)
    return pl.pallas_call(
        q_kernel,
        grid_spec=pltpu.PrefetchScalarGridSpec(
            num_scalar_prefetch=1,
            grid=(1,),
            in_specs=[pl.BlockSpec((1, rows, width), lambda i, p: (p[0], p[1], 0))]
            + [held] * (1 + len(weights)),
            out_specs=pl.BlockSpec((rows, width), lambda i, p: (0, 0)),
        ),
        out_shape=jax.ShapeDtypeStruct((rows, width), jnp.bfloat16),
        name="q_rows",
        compiler_params=pltpu.CompilerParams(vmem_limit_bytes=16 * 1024 * 1024),
        cost_estimate=pl.CostEstimate(
            flops=2 * rows * width * width, bytes_accessed=4 * rows * width, transcendentals=0
        ),
    )(place, state, norms, *weights)


def main_kernel(
    place_ref, near_ref, count_ref, x_ref, norm_ref, q_ref, *rest
):
    kv_refs = rest[:KMAX]
    out_w, up_w, down_w, a_m, b_m, c_m, d_m, a_t, b_t, c_t, d_t = rest[KMAX : KMAX + 11]
    o_ref, heads_ref, resid_ref, up_ref = rest[KMAX + 11 :]
    blk = pl.program_id(0)
    head = NODE_BLK
    scale = math.log2(math.e) / math.sqrt(head)
    count = count_ref[blk]
    rows_at = pl.ds(pl.multiple_of(blk * NODE_BLK, NODE_BLK), NODE_BLK)
    for h in range(HEADS):
        keys = [r[0, :, 2 * h * head : (2 * h + 1) * head] for r in kv_refs]
        vals = [r[0, :, (2 * h + 1) * head : (2 * h + 2) * head] for r in kv_refs]
        query = q_ref[:, h * head : (h + 1) * head]
        scores = lax.dot_general(
            query,
            jnp.concatenate(keys, axis=0),
            (((1,), (1,)), ((), ())),
            preferred_element_type=jnp.float32,
        )
        parts = [
            jnp.where(j < count, scores[:, j * NODE_BLK : (j + 1) * NODE_BLK], -1e30)
            for j in range(KMAX)
        ]
        top = functools.reduce(jnp.maximum, parts)
        top = jnp.max(top, axis=-1, keepdims=True)
        parts = [jnp.exp2((p - top) * scale) for p in parts]
        total = jnp.sum(functools.reduce(jnp.add, parts), axis=-1, keepdims=True)
        mixed = matmul(
            jnp.concatenate([bf(p) for p in parts], axis=1), jnp.concatenate(vals, axis=0)
        )
        heads_ref[rows_at, h * head : (h + 1) * head] = bf(mixed / total)

    @pl.when(blk == pl.num_programs(0) - 1)
    def _():
        width = x_ref.shape[2]
        half = width // 2
        mine = pl.ds(pl.multiple_of(place_ref[2] * half, half), half)
        theirs = pl.ds(pl.multiple_of((1 - place_ref[2]) * half, half), half)
        resid_ref[...] = x_ref[0].astype(jnp.float32) + matmul(heads_ref[:, :head], out_w[...])
        rest_heads = heads_ref[:, head:]
        at = width
        for where, trio in ((mine, (a_m, b_m, c_m)), (theirs, (a_t, b_t, c_t))):
            w = jnp.concatenate([r[at : at + head] for r in trio], axis=0)
            resid_ref[:, where] += matmul(rest_heads, w)
        normed = bf(normalise(resid_ref[...], norm_ref[2:3], norm_ref[3:4]))

        def act(v):
            return bf(0.5 * v * (1.0 + jnp.tanh(0.5 * v)))

        up_ref[:, : width] = act(matmul(normed, up_w[...]))
        for k, r in enumerate((a_m, a_t, b_m, b_t, c_m, c_t)):
            lo = width + k * half
            up_ref[:, lo : lo + half] = act(matmul(normed, r[:width]))
        at = width + head
        lows, highs = [down_w[:, :half]], [down_w[:, half:]]
        for r, base in ((a_m, at), (a_t, at), (b_m, at), (b_t, at), (d_m, 0), (d_t, 0)):
            lows.append(r[base : base + half])
            highs.append(r[base + half : base + 2 * half])
        hidden = up_ref[...]
        resid_ref[:, :half] += matmul(hidden, jnp.concatenate(lows, axis=0))
        resid_ref[:, half:] += matmul(hidden, jnp.concatenate(highs, axis=0))
        for r in range(HEADS):
            col = lax.rem(place_ref[3] + r, HEADS)
            cols = pl.ds(pl.multiple_of(col * head, head), head)
            o_ref[r] = bf(resid_ref[:, cols])


def attend(place, near, count, state, norms, query, kv, weights):
    rows, width = query.shape
    blocks = rows // NODE_BLK
    held = pl.BlockSpec(memory_space=pltpu.VMEM)

    def neighbour(j):
        return pl.BlockSpec(
            (1, NODE_BLK, kv.shape[2]), lambda i, p, n, c: (n[i * KMAX + j], 0, 0)
        )

    return pl.pallas_call(
        main_kernel,
        grid_spec=pltpu.PrefetchScalarGridSpec(
            num_scalar_prefetch=3,
            grid=(blocks,),
            in_specs=[
                pl.BlockSpec((1, rows, width), lambda i, p, n, c: (p[0], p[1], 0)),
                held,
                pl.BlockSpec((NODE_BLK, width), lambda i, p, n, c: (i, 0)),
            ]
            + [neighbour(j) for j in range(KMAX)]
            + [held] * len(weights),
            out_specs=pl.BlockSpec((HEADS, rows, width // HEADS), lambda i, p, n, c: (0, 0, 0)),
            scratch_shapes=[
                pltpu.VMEM((rows, width), jnp.bfloat16),
                pltpu.VMEM((rows, width), jnp.float32),
                pltpu.VMEM((rows, 4 * width), jnp.bfloat16),
            ],
        ),
        out_shape=jax.ShapeDtypeStruct((HEADS, rows, width // HEADS), jnp.bfloat16),
        name="attend_and_mlp",
        compiler_params=pltpu.CompilerParams(vmem_limit_bytes=VMEM_LIMIT),
        cost_estimate=pl.CostEstimate(
            flops=rows * width * (4 * KMAX * NODE_BLK + 2 * width + 16 * width),
            bytes_accessed=16 * 1024 * 1024,
            transcendentals=rows * HEADS * KMAX * NODE_BLK,
        ),
    )(place, near, count, state, norms, query, *([kv] * KMAX), *weights)


def place_kernel(place_ref, own, a, b, c, o_ref):
    rank = place_ref[3]
    for off, r in ((0, own), (3, a), (1, b), (2, c)):
        o_ref[lax.rem(rank + off, HEADS)] = r[...]


def local(
    state, norm_gain, norm_shift, qkv_weight, out_weight, up_weight, down_weight, neighbours, counts
):
    samples, row_count, width = state.shape
    per_dev = row_count // NODE_BLK
    doms = lax.axis_size("dom")
    tps = lax.axis_size("tp")
    dom = lax.axis_index("dom")
    rank = lax.axis_index("tp")
    par = lax.rem(dom, 2)
    per_sample = tps // samples
    sample = rank // per_sample
    share = lax.rem(rank, per_sample)
    rows = row_count // per_sample
    own_blocks = rows // NODE_BLK
    place = jnp.stack([sample, share, par, rank]).astype(jnp.int32)

    def hop(v, pairs):
        return lax.ppermute(v, "dom", pairs)

    def sign(i):
        return 1 if i % 2 == 0 else -1

    def swap(v):
        return hop(v, [(i ^ 1, i) for i in range(doms)])

    def near(v):
        return hop(v, [((i + 2 * sign(i)) % doms, i) for i in range(doms)])

    def far(v):
        return hop(v, [((i - 2 * sign(i)) % doms, i) for i in range(doms)])

    def up(v):
        return lax.ppermute(v, "tp", [(i, (i + 1) % tps) for i in range(tps)])

    def down(v):
        return lax.ppermute(v, "tp", [((i + 1) % tps, i) for i in range(tps)])

    def across(v):
        return lax.ppermute(v, "tp", [(i, (i + 2) % tps) for i in range(tps)])

    qkv = jnp.transpose(qkv_weight, (1, 0, 2))
    w1, w2 = up(qkv), down(qkv)
    mid = width // 2
    w3a, w3b = up(w1[:, :mid]), down(w2[:, mid:])
    qkv_all = (qkv, w1, w2, w3a, w3b)

    own = lax.dynamic_index_in_dim(state, sample, 0, keepdims=False)
    partner = swap(own)
    near_rows = near(own)
    own_late, near_rows = lax.optimization_barrier((own, near_rows))
    far_rows = far(own_late)
    relay = swap(near_rows)

    up_half = lax.dynamic_slice_in_dim(up_weight, par * mid, mid, 1)
    out_half = lax.dynamic_slice_in_dim(out_weight, par * mid, mid, 1)
    down_half = lax.dynamic_slice_in_dim(down_weight, par * mid, mid, 0)
    pack = jnp.concatenate([up_half, out_half, down_half[:, :mid], down_half[:, mid:]], axis=0)
    pack, w1_done, w2_done = lax.optimization_barrier((pack, w1, w2))
    cut = width + NODE_BLK
    a_m, b_m = up(pack), down(pack)
    c_m, d_m = up(a_m[:cut]), down(b_m[cut:])
    a_t, b_t, c_t, d_t = swap(a_m), swap(b_m), swap(c_m), swap(d_m)

    norms = jnp.concatenate(
        [
            lax.dynamic_index_in_dim(v, sample, 1)[i]
            for i in range(2)
            for v in (norm_gain, norm_shift)
        ],
        axis=0,
    )
    slots = 5
    kv = project_kv(own, norms, qkv_all, None, 0, per_dev, slots)
    kv = project_kv(partner, norms, qkv_all, kv, 1, per_dev, slots)
    query = project_q(place, state, norms, qkv_all, rows)
    kv = project_kv(near_rows, norms, qkv_all, kv, 2, per_dev, slots)
    kv = project_kv(relay, norms, qkv_all, kv, 4, per_dev, slots)
    kv = project_kv(far_rows, norms, qkv_all, kv, 3, per_dev, slots)

    listed = lax.dynamic_slice_in_dim(neighbours, share * own_blocks, own_blocks, 0)
    count = lax.dynamic_slice_in_dim(counts, share * own_blocks, own_blocks, 0)
    step = jnp.mod(listed // per_dev - dom + 2, doms) - 2
    slot = jnp.mod(jnp.where(par == 0, step, -step), slots)
    where = (slot * per_dev + jnp.mod(listed, per_dev)).astype(jnp.int32).reshape(-1)

    weights = (out_weight, up_weight, down_weight, a_m, b_m, c_m, d_m, a_t, b_t, c_t, d_t)
    mine = attend(place, where, count, state, norms, query, kv, weights)

    got = (mine[0], up(mine[1]), down(mine[3]), across(mine[2]))
    held = pl.BlockSpec(memory_space=pltpu.VMEM)
    out = pl.pallas_call(
        place_kernel,
        in_specs=[pl.BlockSpec(memory_space=pltpu.SMEM)] + [held] * 4,
        out_specs=held,
        out_shape=jax.ShapeDtypeStruct((tps, rows, width // tps), jnp.bfloat16),
        name="place_rows",
        cost_estimate=pl.CostEstimate(flops=0, bytes_accessed=4 * rows * width, transcendentals=0),
    )(place, *got)
    return out.reshape(samples, row_count, width // tps)


def solution(mesh):
    placed = (
        P(None, "dom", None),
        P(),
        P(),
        P(None, None, "tp"),
        P("tp", None),
        P(None, "tp"),
        P("tp", None),
        P("dom", None),
        P("dom"),
    )
    return jax.shard_map(
        local, mesh=mesh, in_specs=placed, out_specs=P(None, "dom", "tp"), check_vma=False
    )
```

```python
import functools
import math

import jax
import jax.numpy as jnp
from jax import lax
from jax.experimental import pallas as pl
from jax.experimental.pallas import tpu as pltpu
from jax.sharding import PartitionSpec as P

HEADS = 4
NODE_BLK = 128
KMAX = 8
ROWS = 512
MIB = 1024 * 1024

VMEM = pl.BlockSpec(memory_space=pltpu.VMEM)
SMEM = pl.BlockSpec(memory_space=pltpu.SMEM)
ANY = pl.BlockSpec(memory_space=pl.ANY)


def bf(v):
    return v.astype(jnp.bfloat16)


def matmul(a, b):
    return jnp.dot(a, b, preferred_element_type=jnp.float32)


def aligned(i, step):
    return pl.ds(pl.multiple_of(i * step, step), step)


def shape(dims, dtype=jnp.bfloat16):
    return jax.ShapeDtypeStruct(dims, dtype)


def in_hbm(dims, dtype=jnp.bfloat16):
    return pltpu.HBM(dims, dtype)


def cost(flops, nbytes, exps=0):
    return pl.CostEstimate(flops=flops, bytes_accessed=nbytes, transcendentals=exps)


def normalise(values, gain, shift):
    mean = jnp.mean(values, axis=-1, keepdims=True)
    centred = values - mean
    spread = jnp.mean(centred * centred, axis=-1, keepdims=True)
    return centred * lax.rsqrt(spread + 1e-05) * gain + shift


def prepare_kernel(
    place_ref, x_ref, gain_ref, shift_ref, up_ref, out_ref, down_ref, o_ref, pack_ref
):
    s = pl.ds(place_ref[0], 1)
    o_ref[...] = bf(normalise(x_ref[0].astype(jnp.float32), gain_ref[0, s], shift_ref[0, s]))

    @pl.when(pl.program_id(0) == 0)
    def _():
        at = 0
        for r in (up_ref, out_ref, down_ref):
            pack_ref[at : at + r.shape[0]] = r[...]
            at += r.shape[0]


def prepare(place, state, gain, shift, up_w, out_w, down_w):
    _, rows, width = state.shape
    pack_rows = up_w.shape[0] + out_w.shape[0] + down_w.shape[0]
    return pl.pallas_call(
        prepare_kernel,
        grid_spec=pltpu.PrefetchScalarGridSpec(
            num_scalar_prefetch=1,
            grid=(rows // ROWS,),
            in_specs=[pl.BlockSpec((1, ROWS, width), lambda i, p: (p[0], i, 0))] + [VMEM] * 5,
            out_specs=[
                pl.BlockSpec((ROWS, width), lambda i, p: (i, 0)),
                pl.BlockSpec((pack_rows, width), lambda i, p: (0, 0)),
            ],
        ),
        out_shape=[in_hbm((rows, width)), in_hbm((pack_rows, width))],
        name="prepare",
        cost_estimate=cost(10 * rows * width, 4 * (rows + pack_rows) * width),
    )(place, state, gain, shift, up_w, out_w, down_w)


def kv_first_kernel(place_ref, xa, xb, w0, w1, w2, w3m, w3t, kv_ref, q_ref, wkv_ref, wq_ref):
    i = pl.program_id(0)
    head = NODE_BLK
    par = place_ref[2]

    @pl.when(i == 0)
    def _():
        half = w3m.shape[1]
        for h in range(HEADS):
            at = (h // 2) * 4 * head + (h % 2) * head
            spots = ((0, wq_ref, h * head), (1, wkv_ref, at), (2, wkv_ref, at + 2 * head))
            for c, dst, col in spots:
                if h < 3:
                    dst[:, col : col + head] = (w0, w1, w2)[h][c]
                else:
                    dst[aligned(par, half), col : col + head] = w3m[c]
                    dst[aligned(1 - par, half), col : col + head] = w3t[c]

    x = jnp.where(i < 2, xa[...], xb[...])
    kv_ref[...] = bf(matmul(x, wkv_ref[...])).reshape(kv_ref.shape)

    @pl.when(i == place_ref[1])
    def _():
        q_ref[...] = bf(matmul(xa[...], wq_ref[...]))


def kv_first(place, xa, xb, weights):
    rows, width = xa.shape
    steps = rows // ROWS
    per_step = ROWS // NODE_BLK
    blocks = 2 * rows // NODE_BLK
    return pl.pallas_call(
        kv_first_kernel,
        grid_spec=pltpu.PrefetchScalarGridSpec(
            num_scalar_prefetch=1,
            grid=(2 * steps,),
            in_specs=[
                pl.BlockSpec((ROWS, width), lambda i, p: (jnp.minimum(i, steps - 1), 0)),
                pl.BlockSpec((ROWS, width), lambda i, p: (jnp.maximum(i - steps, 0), 0)),
            ]
            + [VMEM] * len(weights),
            out_specs=[
                pl.BlockSpec((per_step, NODE_BLK, 2 * width), lambda i, p: (i, 0, 0)),
                pl.BlockSpec((ROWS, width), lambda i, p: (0, 0)),
                pl.BlockSpec((width, 2 * width), lambda i, p: (0, 0)),
            ],
            scratch_shapes=[pltpu.VMEM((width, width), jnp.bfloat16)],
        ),
        out_shape=[
            in_hbm((blocks, NODE_BLK, 2 * width)),
            shape((ROWS, width)),
            shape((width, 2 * width)),
        ],
        name="kv_first",
        compiler_params=pltpu.CompilerParams(vmem_limit_bytes=24 * MIB),
        cost_estimate=cost(8 * rows * width * width, 8 * MIB),
    )(place, xa, xb, *weights)


def kv_second_kernel(xa, xb, wkv_ref, kv_ref):
    x = jnp.where(pl.program_id(0) < 2, xa[...], xb[...])
    kv_ref[...] = bf(matmul(x, wkv_ref[...])).reshape(kv_ref.shape)


def kv_second(xa, xb, wkv):
    rows, width = xa.shape
    steps = rows // ROWS
    per_step = ROWS // NODE_BLK
    blocks = 2 * rows // NODE_BLK
    return pl.pallas_call(
        kv_second_kernel,
        grid=(2 * steps,),
        in_specs=[
            pl.BlockSpec((ROWS, width), lambda i: (jnp.minimum(i, steps - 1), 0)),
            pl.BlockSpec((ROWS, width), lambda i: (jnp.maximum(i - steps, 0), 0)),
            VMEM,
        ],
        out_specs=pl.BlockSpec((per_step, NODE_BLK, 2 * width), lambda i: (i, 0, 0)),
        out_shape=in_hbm((blocks, NODE_BLK, 2 * width)),
        name="kv_second",
        compiler_params=pltpu.CompilerParams(vmem_limit_bytes=24 * MIB),
        cost_estimate=cost(8 * rows * width * width, 7 * MIB),
    )(xa, xb, wkv)


def main_kernel(
    place_ref, list_ref, count_ref, far_ref, gain_ref, shift_ref, q_ref, wkv_ref,
    kv_a, kv_b, state_ref, out_w, up_w, down_w, p1, p1s, p2, p2s,
    o0, o1, o2, o3,
    kv, rows_in, wall, heads_ref, resid_ref, hidden_ref, sems, *, doms, per_dev,
):
    sample, share, par, rank, dom = [place_ref[k] for k in range(5)]
    head = NODE_BLK
    rows, width = q_ref.shape
    half_pack = p2.shape[0]
    early = kv_a.shape[0]
    jobs = [
        (kv_a, kv.at[pl.ds(0, early)]),
        (kv_b, kv.at[pl.ds(early, early)]),
        (state_ref.at[sample, aligned(share, rows)], rows_in),
        (out_w, wall.at[0, pl.ds(width, head)]),
        (up_w, wall.at[0, pl.ds(0, width)]),
        (down_w, wall.at[0, pl.ds(width + head, width)]),
        (p1, wall.at[1]),
        (p1s, wall.at[2]),
        (p2, wall.at[3, aligned(par, half_pack)]),
        (p2s, wall.at[3, aligned(1 - par, half_pack)]),
    ]
    copies = [pltpu.make_async_copy(a, b, sems.at[k]) for k, (a, b) in enumerate(jobs)]
    for c in copies:
        c.start()

    kv[2 * early :] = bf(matmul(far_ref[...], wkv_ref[...])).reshape(
        (per_dev, NODE_BLK, 2 * width)
    )
    for c in copies[:2]:
        c.wait()

    scale = math.log2(math.e) / math.sqrt(head)
    blocks = rows // NODE_BLK
    for b in range(blocks):
        row = share * blocks + b
        count = count_ref[row]
        where = []
        for j in range(KMAX):
            entry = list_ref[row, j]
            part = lax.div(entry, per_dev)
            step = lax.rem(part - dom + (doms + 2), doms) - 2
            turned = jnp.where(par == 0, step, -step)
            slot = jnp.where(
                turned >= 0, jnp.where(turned == 0, 0, turned), jnp.where(turned == -1, 3, 4)
            )
            where.append(slot * per_dev + lax.rem(entry, per_dev))
        at = slice(b * NODE_BLK, (b + 1) * NODE_BLK)
        for pair in range(HEADS // 2):
            col = pair * 4 * head
            keys = jnp.concatenate([kv[i, :, col : col + 2 * head] for i in where], axis=0)
            vals = jnp.concatenate(
                [kv[i, :, col + 2 * head : col + 4 * head] for i in where], axis=0
            )
            q0 = q_ref[at, 2 * pair * head : (2 * pair + 1) * head]
            q1 = q_ref[at, (2 * pair + 1) * head : (2 * pair + 2) * head]
            zero = jnp.zeros_like(q0)
            query = jnp.concatenate(
                [jnp.concatenate([q0, zero], axis=1), jnp.concatenate([zero, q1], axis=1)], axis=0
            )
            scores = lax.dot_general(
                query, keys, (((1,), (1,)), ((), ())), preferred_element_type=jnp.float32
            )
            parts = [
                jnp.where(j < count, scores[:, j * NODE_BLK : (j + 1) * NODE_BLK], -1e30)
                for j in range(KMAX)
            ]
            top = jnp.max(functools.reduce(jnp.maximum, parts), axis=-1, keepdims=True)
            parts = [jnp.exp2((p - top) * scale) for p in parts]
            total = jnp.sum(functools.reduce(jnp.add, parts), axis=-1, keepdims=True)
            mixed = matmul(jnp.concatenate([bf(p) for p in parts], axis=1), vals) / total
            heads_ref[at, 2 * pair * head : (2 * pair + 1) * head] = bf(mixed[:head, :head])
            heads_ref[at, (2 * pair + 1) * head : (2 * pair + 2) * head] = bf(mixed[head:, head:])

    for c in copies[2:]:
        c.wait()
    out_all = jnp.concatenate([wall[h, width : width + head] for h in range(HEADS)], axis=0)
    resid_ref[...] = rows_in[...].astype(jnp.float32) + matmul(heads_ref[...], out_all)
    s = pl.ds(sample, 1)
    normed = bf(normalise(resid_ref[...], gain_ref[1, s], shift_ref[1, s]))
    for h in range(HEADS):
        v = matmul(normed, wall[h, :width])
        hidden_ref[:, h * width : (h + 1) * width] = bf(0.5 * v * (1.0 + jnp.tanh(0.5 * v)))
    down_all = jnp.concatenate([wall[h, width + head :] for h in range(HEADS)], axis=0)
    resid_ref[...] += matmul(hidden_ref[...], down_all)
    for r, o_ref in enumerate((o0, o1, o2, o3)):
        o_ref[...] = bf(resid_ref[:, aligned(lax.rem(rank + r, HEADS), head)])


def attend(place, listed, counts, far, gain, shift, query, wkv, arrays, per_dev, doms):
    rows, width = query.shape
    head = NODE_BLK
    pack_rows = 2 * width + head
    return pl.pallas_call(
        functools.partial(main_kernel, doms=doms, per_dev=per_dev),
        in_specs=[SMEM] * 3 + [VMEM] * 5 + [ANY] * len(arrays),
        out_specs=[VMEM] * HEADS,
        out_shape=[shape((rows, head))] * HEADS,
        scratch_shapes=[
            pltpu.VMEM((5 * per_dev, NODE_BLK, 2 * width), jnp.bfloat16),
            pltpu.VMEM((rows, width), jnp.bfloat16),
            pltpu.VMEM((HEADS, pack_rows, width), jnp.bfloat16),
            pltpu.VMEM((rows, width), jnp.bfloat16),
            pltpu.VMEM((rows, width), jnp.float32),
            pltpu.VMEM((rows, HEADS * width), jnp.bfloat16),
            pltpu.SemaphoreType.DMA((10,)),
        ],
        name="attend_and_mlp",
        compiler_params=pltpu.CompilerParams(vmem_limit_bytes=48 * MIB),
        cost_estimate=cost(
            rows * width * (4 * KMAX * NODE_BLK + 2 * width + 16 * width) + 4 * rows * width**2,
            16 * MIB,
            rows * HEADS * KMAX * NODE_BLK,
        ),
    )(place, listed, counts, far, gain, shift, query, wkv, *arrays)


def place_kernel(place_ref, own, a, b, c, o_ref):
    rank = place_ref[3]
    for off, r in ((0, own), (3, a), (1, b), (2, c)):
        o_ref[lax.rem(rank + off, HEADS)] = r[...]


def placed_rows(place, pieces):
    rows, head = pieces[0].shape
    return pl.pallas_call(
        place_kernel,
        in_specs=[SMEM] + [VMEM] * HEADS,
        out_specs=VMEM,
        out_shape=shape((HEADS, rows, head)),
        name="place_rows",
        compiler_params=pltpu.CompilerParams(vmem_limit_bytes=4 * MIB),
        cost_estimate=cost(0, 16 * rows * head),
    )(place, *pieces)


def after(value, *deps):
    return lax.optimization_barrier((value, *deps))[0]


def local(
    state, norm_gain, norm_shift, qkv_weight, out_weight, up_weight, down_weight, neighbours, counts
):
    samples, row_count, width = state.shape
    per_dev = row_count // NODE_BLK
    doms = lax.axis_size("dom")
    tps = lax.axis_size("tp")
    dom = lax.axis_index("dom")
    rank = lax.axis_index("tp")
    par = lax.rem(dom, 2)
    per_sample = tps // samples
    place = jnp.stack([rank // per_sample, lax.rem(rank, per_sample), par, rank, dom])
    place = place.astype(jnp.int32)

    def hop(v, pairs):
        return lax.ppermute(v, "dom", pairs)

    def sign(i):
        return 1 if i % 2 == 0 else -1

    def swap(v):
        return hop(v, [(i ^ 1, i) for i in range(doms)])

    def near(v):
        return hop(v, [((i + 2 * sign(i)) % doms, i) for i in range(doms)])

    def far(v):
        return hop(v, [((i - 2 * sign(i)) % doms, i) for i in range(doms)])

    def ring(v):
        pairs = [
            (i * tps + (t - sign(i)) % tps, i * tps + t) for i in range(doms) for t in range(tps)
        ]
        return lax.ppermute(v, ("dom", "tp"), pairs)

    def up(v):
        return lax.ppermute(v, "tp", [(i, (i + 1) % tps) for i in range(tps)])

    def down(v):
        return lax.ppermute(v, "tp", [((i + 1) % tps, i) for i in range(tps)])

    def across(v):
        return lax.ppermute(v, "tp", [(i, (i + 2) % tps) for i in range(tps)])

    qkv = jnp.transpose(qkv_weight, (1, 0, 2))
    w1 = ring(qkv)
    own, pack = prepare(
        place, state, norm_gain, norm_shift, up_weight, out_weight, down_weight
    )
    near_rows = near(own)
    partner = swap(own)

    w1 = after(w1, own)
    w2 = swap(w1)
    mid = width // 2
    w1_half = lax.dynamic_slice_in_dim(w1, par * mid, mid, 1)
    w3m = ring(w1_half)
    w3t = swap(w3m)
    p1 = ring(after(pack, w1_half))

    kv_a, query, wkv = kv_first(place, own, partner, (qkv, w1, w2, w3m, w3t))
    far_rows = far(after(own, near_rows))
    relay = swap(near_rows)
    mid = pack.shape[0] // 2
    p1s = swap(p1)
    p2 = ring(lax.dynamic_slice_in_dim(p1, par * mid, mid, 0))
    p2s = swap(p2)
    kv_b = kv_second(near_rows, relay, wkv)

    mine = attend(
        place, neighbours, counts, far_rows, norm_gain, norm_shift, query, wkv,
        (kv_a, kv_b, state, out_weight, up_weight, down_weight, p1, p1s, p2, p2s),
        per_dev, doms,
    )
    out = placed_rows(place, (mine[0], up(mine[1]), down(mine[3]), across(mine[2])))
    return out.reshape(samples, row_count, width // tps)


def solution(mesh):
    placed = (
        P(None, "dom", None),
        P(),
        P(),
        P(None, None, "tp"),
        P("tp", None),
        P(None, "tp"),
        P("tp", None),
        P("dom", None),
        P("dom"),
    )
    return jax.shard_map(
        local, mesh=mesh, in_specs=placed, out_specs=P(None, "dom", "tp"), check_vma=False
    )
```

```python
import functools
import math

import jax
import jax.numpy as jnp
from jax import lax
from jax.experimental import pallas as pl
from jax.experimental.pallas import tpu as pltpu
from jax.sharding import PartitionSpec as P

HEADS = 4
NODE_BLK = 128
KMAX = 8
ROWS = 512
MIB = 1024 * 1024

VMEM = pl.BlockSpec(memory_space=pltpu.VMEM)
SMEM = pl.BlockSpec(memory_space=pltpu.SMEM)
HBM = pl.BlockSpec(memory_space=pltpu.HBM)


def bf(v):
    return v.astype(jnp.bfloat16)


def matmul(a, b):
    return jnp.dot(a, b, preferred_element_type=jnp.float32)


def aligned(i, step):
    return pl.ds(pl.multiple_of(i * step, step), step)


def shape(dims, dtype=jnp.bfloat16):
    return jax.ShapeDtypeStruct(dims, dtype)


def in_hbm(dims, dtype=jnp.bfloat16):
    return pltpu.HBM(dims, dtype)


def cost(flops, nbytes, exps=0):
    return pl.CostEstimate(flops=flops, bytes_accessed=nbytes, transcendentals=exps)


def normalise(values, gain, shift):
    mean = jnp.mean(values, axis=-1, keepdims=True)
    centred = values - mean
    spread = jnp.mean(centred * centred, axis=-1, keepdims=True)
    return centred * lax.rsqrt(spread + 1e-05) * gain + shift


def my_place():
    dom = lax.axis_index("dom")
    rank = lax.axis_index("tp")
    return lax.div(rank, 2), lax.rem(rank, 2), lax.rem(dom, 2), rank, dom


def norm_kernel(state_ref, gain_ref, shift_ref, o_ref, x_in, x_out, sems):
    sample = my_place()[0]
    s = pl.ds(sample, 1)
    chunks = sems.shape[1]
    step = x_in.shape[0] // chunks
    spans = [pl.ds(k * step, step) for k in range(chunks)]
    loads = [
        pltpu.make_async_copy(state_ref.at[sample, at], x_in.at[at], sems.at[0, k])
        for k, at in enumerate(spans)
    ]
    stores = [
        pltpu.make_async_copy(x_out.at[at], o_ref.at[at], sems.at[1, k])
        for k, at in enumerate(spans)
    ]
    for c in loads:
        c.start()
    gain, shift = gain_ref[0, s], shift_ref[0, s]
    for k, at in enumerate(spans):
        loads[k].wait()
        x_out[at] = bf(normalise(x_in[at].astype(jnp.float32), gain, shift))
        stores[k].start()
    for c in stores:
        c.wait()


def normed_rows(state, gain, shift):
    _, rows, width = state.shape
    return pl.pallas_call(
        norm_kernel,
        in_specs=[HBM, VMEM, VMEM],
        out_specs=HBM,
        out_shape=in_hbm((rows, width)),
        scratch_shapes=[
            pltpu.VMEM((rows, width), jnp.bfloat16),
            pltpu.VMEM((rows, width), jnp.bfloat16),
            pltpu.SemaphoreType.DMA((2, 8)),
        ],
        name="norm_rows",
        compiler_params=pltpu.CompilerParams(vmem_limit_bytes=24 * MIB),
        cost_estimate=cost(10 * rows * width, 4 * rows * width),
    )(state, gain, shift)


def pack_kernel(up_ref, out_ref, down_ref, o_ref):
    at = 0
    for r in (up_ref, out_ref, down_ref):
        o_ref[at : at + r.shape[0]] = r[...]
        at += r.shape[0]


def packed(up_w, out_w, down_w):
    rows = up_w.shape[0] + out_w.shape[0] + down_w.shape[0]
    return pl.pallas_call(
        pack_kernel,
        in_specs=[VMEM] * 3,
        out_specs=VMEM,
        out_shape=in_hbm((rows, up_w.shape[1])),
        name="pack_weights",
        compiler_params=pltpu.CompilerParams(vmem_limit_bytes=8 * MIB),
        cost_estimate=cost(0, 4 * rows * up_w.shape[1]),
    )(up_w, out_w, down_w)


def kv_first_kernel(xa, xb, w0, w1, w2, w3m, w3t, kv_ref, q_ref, wkv_ref, wq_ref):
    i = pl.program_id(0)
    head = NODE_BLK
    _, share, par, _, _ = my_place()

    @pl.when(i == 0)
    def _():
        half = w3m.shape[1]
        for h in range(HEADS):
            at = (h // 2) * 4 * head + (h % 2) * head
            spots = ((0, wq_ref, h * head), (1, wkv_ref, at), (2, wkv_ref, at + 2 * head))
            for c, dst, col in spots:
                if h < 3:
                    dst[:, col : col + head] = (w0, w1, w2)[h][c]
                else:
                    dst[aligned(par, half), col : col + head] = w3m[c]
                    dst[aligned(1 - par, half), col : col + head] = w3t[c]

    x = jnp.where(i < 2, xa[...], xb[...])
    kv_ref[...] = bf(matmul(x, wkv_ref[...])).reshape(kv_ref.shape)

    @pl.when(i == share)
    def _():
        q_ref[...] = bf(matmul(xa[...], wq_ref[...]))


def kv_first(xa, xb, weights):
    rows, width = xa.shape
    steps = rows // ROWS
    per_step = ROWS // NODE_BLK
    blocks = 2 * rows // NODE_BLK
    return pl.pallas_call(
        kv_first_kernel,
        grid=(2 * steps,),
        in_specs=[
            pl.BlockSpec((ROWS, width), lambda i: (jnp.minimum(i, steps - 1), 0)),
            pl.BlockSpec((ROWS, width), lambda i: (jnp.maximum(i - steps, 0), 0)),
        ]
        + [VMEM] * len(weights),
        out_specs=[
            pl.BlockSpec((per_step, NODE_BLK, 2 * width), lambda i: (i, 0, 0)),
            pl.BlockSpec((ROWS, width), lambda i: (0, 0)),
            pl.BlockSpec((width, 2 * width), lambda i: (0, 0)),
        ],
        scratch_shapes=[pltpu.VMEM((width, width), jnp.bfloat16)],
        out_shape=[
            in_hbm((blocks, NODE_BLK, 2 * width)),
            shape((ROWS, width)),
            shape((width, 2 * width)),
        ],
        name="kv_first",
        compiler_params=pltpu.CompilerParams(vmem_limit_bytes=24 * MIB),
        cost_estimate=cost(8 * rows * width * width, 8 * MIB),
    )(xa, xb, *weights)


def kv_second_kernel(xa, xb, wkv_ref, kv_ref):
    x = jnp.where(pl.program_id(0) < 2, xa[...], xb[...])
    kv_ref[...] = bf(matmul(x, wkv_ref[...])).reshape(kv_ref.shape)


def kv_second(xa, xb, wkv):
    rows, width = xa.shape
    steps = rows // ROWS
    per_step = ROWS // NODE_BLK
    blocks = 2 * rows // NODE_BLK
    return pl.pallas_call(
        kv_second_kernel,
        grid=(2 * steps,),
        in_specs=[
            pl.BlockSpec((ROWS, width), lambda i: (jnp.minimum(i, steps - 1), 0)),
            pl.BlockSpec((ROWS, width), lambda i: (jnp.maximum(i - steps, 0), 0)),
            VMEM,
        ],
        out_specs=pl.BlockSpec((per_step, NODE_BLK, 2 * width), lambda i: (i, 0, 0)),
        out_shape=in_hbm((blocks, NODE_BLK, 2 * width)),
        name="kv_second",
        compiler_params=pltpu.CompilerParams(vmem_limit_bytes=24 * MIB),
        cost_estimate=cost(8 * rows * width * width, 7 * MIB),
    )(xa, xb, wkv)


def attend_kernel(
    list_ref, count_ref, far_ref, q_ref, wkv_ref, kv_a, kv_b, heads_ref, kv, sems, *, doms, per_dev
):
    _, share, par, _, dom = my_place()
    head = NODE_BLK
    rows, width = q_ref.shape
    early = kv_a.shape[0]
    copies = [
        pltpu.make_async_copy(kv_a, kv.at[pl.ds(0, early)], sems.at[0]),
        pltpu.make_async_copy(kv_b, kv.at[pl.ds(early, early)], sems.at[1]),
    ]
    for c in copies:
        c.start()

    kv[2 * early :] = bf(matmul(far_ref[...], wkv_ref[...])).reshape(
        (per_dev, NODE_BLK, 2 * width)
    )
    for c in copies:
        c.wait()

    scale = math.log2(math.e) / math.sqrt(head)
    blocks = rows // NODE_BLK
    for b in range(blocks):
        row = share * blocks + b
        count = count_ref[row]
        where = []
        for j in range(KMAX):
            entry = list_ref[row, j]
            part = lax.div(entry, per_dev)
            step = lax.rem(part - dom + (doms + 2), doms) - 2
            turned = jnp.where(par == 0, step, -step)
            slot = jnp.where(
                turned >= 0, jnp.where(turned == 0, 0, turned), jnp.where(turned == -1, 3, 4)
            )
            where.append(slot * per_dev + lax.rem(entry, per_dev))
        at = slice(b * NODE_BLK, (b + 1) * NODE_BLK)
        for pair in range(HEADS // 2):
            col = pair * 4 * head
            keys = jnp.concatenate([kv[i, :, col : col + 2 * head] for i in where], axis=0)
            vals = jnp.concatenate(
                [kv[i, :, col + 2 * head : col + 4 * head] for i in where], axis=0
            )
            q0 = q_ref[at, 2 * pair * head : (2 * pair + 1) * head]
            q1 = q_ref[at, (2 * pair + 1) * head : (2 * pair + 2) * head]
            zero = jnp.zeros_like(q0)
            query = jnp.concatenate(
                [jnp.concatenate([q0, zero], axis=1), jnp.concatenate([zero, q1], axis=1)], axis=0
            )
            scores = lax.dot_general(
                query, keys, (((1,), (1,)), ((), ())), preferred_element_type=jnp.float32
            )
            parts = [
                jnp.where(j < count, scores[:, j * NODE_BLK : (j + 1) * NODE_BLK], -1e30)
                for j in range(KMAX)
            ]
            top = jnp.max(functools.reduce(jnp.maximum, parts), axis=-1, keepdims=True)
            parts = [jnp.exp2((p - top) * scale) for p in parts]
            total = jnp.sum(functools.reduce(jnp.add, parts), axis=-1, keepdims=True)
            mixed = matmul(jnp.concatenate([bf(p) for p in parts], axis=1), vals) / total
            heads_ref[at, 2 * pair * head : (2 * pair + 1) * head] = bf(mixed[:head, :head])
            heads_ref[at, (2 * pair + 1) * head : (2 * pair + 2) * head] = bf(mixed[head:, head:])


def attend(listed, counts, far, query, wkv, kv_a, kv_b, per_dev, doms):
    rows, width = query.shape
    return pl.pallas_call(
        functools.partial(attend_kernel, doms=doms, per_dev=per_dev),
        in_specs=[SMEM] * 2 + [VMEM] * 3 + [HBM] * 2,
        out_specs=VMEM,
        out_shape=shape((rows, width)),
        scratch_shapes=[
            pltpu.VMEM((5 * per_dev, NODE_BLK, 2 * width), jnp.bfloat16),
            pltpu.SemaphoreType.DMA((2,)),
        ],
        name="attend",
        compiler_params=pltpu.CompilerParams(vmem_limit_bytes=32 * MIB),
        cost_estimate=cost(
            4 * rows * width * KMAX * NODE_BLK + 4 * rows * width**2,
            10 * MIB,
            rows * HEADS * KMAX * NODE_BLK,
        ),
    )(listed, counts, far, query, wkv, kv_a, kv_b)


def mlp_kernel(
    heads_ref, gain_ref, shift_ref, out_w, up_w, down_w, p1, p1s, p2, p2s, state_ref,
    o0, o1, o2, o3,
    rows_in, last, resid_ref, hidden_ref, sem,
):
    sample, share, par, rank, _ = my_place()
    head = NODE_BLK
    rows, width = heads_ref.shape
    copy = pltpu.make_async_copy(state_ref.at[sample, aligned(share, rows)], rows_in, sem)
    copy.start()
    half = p2.shape[0]
    last[aligned(par, half)] = p2[...]
    last[aligned(1 - par, half)] = p2s[...]
    packs = (p1, p1s, last)
    out_all = jnp.concatenate([out_w[...]] + [p[width : width + head] for p in packs], axis=0)
    mixed = matmul(heads_ref[...], out_all)
    copy.wait()
    resid_ref[...] = rows_in[...].astype(jnp.float32) + mixed
    s = pl.ds(sample, 1)
    normed = bf(normalise(resid_ref[...], gain_ref[1, s], shift_ref[1, s]))
    for h in range(HEADS):
        v = matmul(normed, up_w[...] if h == 0 else packs[h - 1][:width])
        hidden_ref[:, h * width : (h + 1) * width] = bf(0.5 * v * (1.0 + jnp.tanh(0.5 * v)))
    down_all = jnp.concatenate([down_w[...]] + [p[width + head :] for p in packs], axis=0)
    resid_ref[...] += matmul(hidden_ref[...], down_all)
    for r, o_ref in enumerate((o0, o1, o2, o3)):
        o_ref[...] = bf(resid_ref[:, aligned(lax.rem(rank + r, HEADS), head)])


def mlp(heads, gain, shift, weights, state):
    rows, width = heads.shape
    head = NODE_BLK
    return pl.pallas_call(
        mlp_kernel,
        in_specs=[VMEM] * (3 + len(weights)) + [HBM],
        out_specs=[VMEM] * HEADS,
        out_shape=[shape((rows, head))] * HEADS,
        scratch_shapes=[
            pltpu.VMEM((rows, width), jnp.bfloat16),
            pltpu.VMEM((2 * width + head, width), jnp.bfloat16),
            pltpu.VMEM((rows, width), jnp.float32),
            pltpu.VMEM((rows, HEADS * width), jnp.bfloat16),
            pltpu.SemaphoreType.DMA,
        ],
        name="mlp",
        compiler_params=pltpu.CompilerParams(vmem_limit_bytes=24 * MIB),
        cost_estimate=cost(18 * rows * width * width, 8 * MIB, rows * HEADS * width),
    )(heads, gain, shift, *weights, state)


def place_kernel(own, a, b, c, o_ref):
    rank = my_place()[3]
    for off, r in ((0, own), (3, a), (1, b), (2, c)):
        o_ref[lax.rem(rank + off, HEADS)] = r[...]


def placed_rows(pieces):
    rows, head = pieces[0].shape
    return pl.pallas_call(
        place_kernel,
        in_specs=[VMEM] * HEADS,
        out_specs=VMEM,
        out_shape=shape((HEADS, rows, head)),
        name="place_rows",
        compiler_params=pltpu.CompilerParams(vmem_limit_bytes=4 * MIB),
        cost_estimate=cost(0, 16 * rows * head),
    )(*pieces)


def after(value, *deps):
    return lax.optimization_barrier((value, *deps))[0]


def local(
    state, norm_gain, norm_shift, qkv_weight, out_weight, up_weight, down_weight, neighbours, counts
):
    samples, row_count, width = state.shape
    per_dev = row_count // NODE_BLK
    doms = lax.axis_size("dom")
    tps = lax.axis_size("tp")
    dom = lax.axis_index("dom")
    par = lax.rem(dom, 2)

    def hop(v, pairs):
        return lax.ppermute(v, "dom", pairs)

    def sign(i):
        return 1 if i % 2 == 0 else -1

    def swap(v):
        return hop(v, [(i ^ 1, i) for i in range(doms)])

    def near(v):
        return hop(v, [((i + 2 * sign(i)) % doms, i) for i in range(doms)])

    def far(v):
        return hop(v, [((i - 2 * sign(i)) % doms, i) for i in range(doms)])

    def ring(v):
        pairs = [
            (i * tps + (t - sign(i)) % tps, i * tps + t) for i in range(doms) for t in range(tps)
        ]
        return lax.ppermute(v, ("dom", "tp"), pairs)

    def up(v):
        return lax.ppermute(v, "tp", [(i, (i + 1) % tps) for i in range(tps)])

    def down(v):
        return lax.ppermute(v, "tp", [((i + 1) % tps, i) for i in range(tps)])

    def across(v):
        return lax.ppermute(v, "tp", [(i, (i + 2) % tps) for i in range(tps)])

    qkv = jnp.transpose(qkv_weight, (1, 0, 2))
    w1 = ring(qkv)
    own = normed_rows(state, norm_gain, norm_shift)
    near_rows = near(own)
    partner = swap(own)
    pack = packed(after(up_weight, own), out_weight, down_weight)

    w1 = after(w1, own)
    w2 = swap(w1)
    mid = width // 2
    w1_half = lax.dynamic_slice_in_dim(w1, par * mid, mid, 1)
    w3m = ring(w1_half)
    w3t = swap(w3m)
    p1 = ring(after(pack, w1_half))

    own_late, near_rows = lax.optimization_barrier((own, near_rows))
    far_rows = far(own_late)
    relay = swap(near_rows)
    kv_a, query, wkv = kv_first(own_late, partner, (qkv, w1, w2, w3m, w3t))
    mid = pack.shape[0] // 2
    p1 = after(p1, query)
    p1s = swap(p1)
    p2 = ring(lax.dynamic_slice_in_dim(p1, par * mid, mid, 0))
    kv_b = kv_second(near_rows, relay, wkv)
    p2 = after(p2, kv_b)
    p2s = swap(p2)

    heads = attend(neighbours, counts, far_rows, query, wkv, kv_a, kv_b, per_dev, doms)
    weights = (out_weight, up_weight, down_weight, p1, p1s, p2, p2s)
    mine = mlp(heads, norm_gain, norm_shift, weights, state)
    out = placed_rows((mine[0], up(mine[1]), down(mine[3]), across(mine[2])))
    return out.reshape(samples, row_count, width // tps)


def solution(mesh):
    placed = (
        P(None, "dom", None),
        P(),
        P(),
        P(None, None, "tp"),
        P("tp", None),
        P(None, "tp"),
        P("tp", None),
        P("dom", None),
        P("dom"),
    )
    return jax.shard_map(
        local, mesh=mesh, in_specs=placed, out_specs=P(None, "dom", "tp"), check_vma=False
    )
```

```python
import functools
import math

import jax
import jax.numpy as jnp
from jax import lax
from jax.experimental import pallas as pl
from jax.experimental.pallas import tpu as pltpu
from jax.sharding import PartitionSpec as P

HEADS = 4
NODE_BLK = 128
KMAX = 8
ROWS = 512
MIB = 1024 * 1024

VMEM = pl.BlockSpec(memory_space=pltpu.VMEM)
SMEM = pl.BlockSpec(memory_space=pltpu.SMEM)
HBM = pl.BlockSpec(memory_space=pltpu.HBM)


def bf(v):
    return v.astype(jnp.bfloat16)


def matmul(a, b):
    return jnp.dot(a, b, preferred_element_type=jnp.float32)


def aligned(i, step):
    return pl.ds(pl.multiple_of(i * step, step), step)


def shape(dims, dtype=jnp.bfloat16):
    return jax.ShapeDtypeStruct(dims, dtype)


def in_hbm(dims, dtype=jnp.bfloat16):
    return pltpu.HBM(dims, dtype)


def in_vmem(dims, dtype=jnp.bfloat16):
    return pltpu.VMEM(dims, dtype)


def kept_in_hbm(v):
    return pltpu.with_memory_space_constraint(v, pltpu.HBM)


def cost(flops, nbytes, exps=0):
    return pl.CostEstimate(flops=flops, bytes_accessed=nbytes, transcendentals=exps)


def normalise(values, gain, shift):
    mean = jnp.mean(values, axis=-1, keepdims=True)
    centred = values - mean
    spread = jnp.mean(centred * centred, axis=-1, keepdims=True)
    return centred * lax.rsqrt(spread + 1e-05) * gain + shift


def my_place():
    dom = lax.axis_index("dom")
    rank = lax.axis_index("tp")
    return lax.div(rank, 2), lax.rem(rank, 2), lax.rem(dom, 2), rank, dom


def norm_kernel(state_ref, gain_ref, shift_ref, o_ref, x_in, affine, sems):
    sample = my_place()[0]
    s = pl.ds(sample, 1)
    chunks = sems.shape[0] - 2
    step = x_in.shape[0] // chunks
    spans = [pl.ds(k * step, step) for k in range(chunks)]
    loads = [
        pltpu.make_async_copy(state_ref.at[sample, at], x_in.at[at], sems.at[k])
        for k, at in enumerate(spans)
    ]
    small = [
        pltpu.make_async_copy(r, affine.at[k], sems.at[chunks + k])
        for k, r in enumerate((gain_ref, shift_ref))
    ]
    for c in loads[:1] + small + loads[1:]:
        c.start()
    for c in small:
        c.wait()
    gain, shift = affine[0, 0, s], affine[1, 0, s]
    for c, at in zip(loads, spans):
        c.wait()
        o_ref[at] = bf(normalise(x_in[at].astype(jnp.float32), gain, shift))


def normed_rows(state, gain, shift):
    _, rows, width = state.shape
    return pl.pallas_call(
        norm_kernel,
        in_specs=[HBM] * 3,
        out_specs=VMEM,
        out_shape=in_vmem((rows, width)),
        scratch_shapes=[
            pltpu.VMEM((rows, width), jnp.bfloat16),
            pltpu.VMEM((2, *gain.shape), jnp.float32),
            pltpu.SemaphoreType.DMA((6,)),
        ],
        name="norm_rows",
        compiler_params=pltpu.CompilerParams(vmem_limit_bytes=8 * MIB),
        cost_estimate=cost(10 * rows * width, 4 * rows * width),
    )(kept_in_hbm(state), kept_in_hbm(gain), kept_in_hbm(shift))


def pack_kernel(up_ref, out_ref, down_ref, o_ref):
    at = 0
    for r in (up_ref, out_ref, down_ref):
        o_ref[at : at + r.shape[0]] = r[...]
        at += r.shape[0]


def packed(up_w, out_w, down_w):
    rows = up_w.shape[0] + out_w.shape[0] + down_w.shape[0]
    return pl.pallas_call(
        pack_kernel,
        in_specs=[VMEM] * 3,
        out_specs=VMEM,
        out_shape=in_hbm((rows, up_w.shape[1])),
        name="pack_weights",
        compiler_params=pltpu.CompilerParams(vmem_limit_bytes=8 * MIB),
        cost_estimate=cost(0, 4 * rows * up_w.shape[1]),
    )(up_w, out_w, down_w)


def write_kv(x_ref, wkv_ref, kv_ref, first):
    rows, width = x_ref.shape
    for r in range(0, rows, ROWS):
        out = bf(matmul(x_ref[r : r + ROWS], wkv_ref[...]))
        at = first + r // NODE_BLK
        kv_ref[at : at + ROWS // NODE_BLK] = out.reshape((ROWS // NODE_BLK, NODE_BLK, 2 * width))


def kv_first_kernel(xa, xb, w0, w1, w2, w3m, w3t, kv_ref, q_ref, wkv_ref, wq_ref):
    head = NODE_BLK
    _, share, par, _, _ = my_place()
    half = w3m.shape[1]
    for h in range(HEADS):
        at = (h // 2) * 4 * head + (h % 2) * head
        spots = ((0, wq_ref, h * head), (1, wkv_ref, at), (2, wkv_ref, at + 2 * head))
        for c, dst, col in spots:
            if h < 3:
                dst[:, col : col + head] = (w0, w1, w2)[h][c]
            else:
                dst[aligned(par, half), col : col + head] = w3m[c]
                dst[aligned(1 - par, half), col : col + head] = w3t[c]
    write_kv(xa, wkv_ref, kv_ref, 0)
    write_kv(xb, wkv_ref, kv_ref, xa.shape[0] // NODE_BLK)
    q_ref[...] = bf(matmul(xa[aligned(share, q_ref.shape[0])], wq_ref[...]))


def kv_first(xa, xb, weights, slots):
    rows, width = xa.shape
    return pl.pallas_call(
        kv_first_kernel,
        in_specs=[VMEM] * (2 + len(weights)),
        out_specs=[VMEM] * 3,
        scratch_shapes=[pltpu.VMEM((width, width), jnp.bfloat16)],
        out_shape=[
            in_vmem((slots * rows // NODE_BLK, NODE_BLK, 2 * width)),
            in_vmem((rows // 2, width)),
            in_vmem((width, 2 * width)),
        ],
        name="kv_first",
        compiler_params=pltpu.CompilerParams(vmem_limit_bytes=16 * MIB),
        cost_estimate=cost(8 * rows * width * width, 8 * MIB),
    )(xa, xb, *weights)


def kv_second_kernel(xa, xb, wkv_ref, kv_in, kv_ref):
    first = 2 * xa.shape[0] // NODE_BLK
    write_kv(xa, wkv_ref, kv_ref, first)
    write_kv(xb, wkv_ref, kv_ref, first + xa.shape[0] // NODE_BLK)


def kv_second(xa, xb, wkv, kv):
    rows, width = xa.shape
    return pl.pallas_call(
        kv_second_kernel,
        in_specs=[VMEM] * 4,
        out_specs=VMEM,
        out_shape=in_vmem(kv.shape),
        input_output_aliases={3: 0},
        name="kv_second",
        compiler_params=pltpu.CompilerParams(vmem_limit_bytes=16 * MIB),
        cost_estimate=cost(8 * rows * width * width, 7 * MIB),
    )(xa, xb, wkv, kv)


def attend_kernel(
    list_ref, count_ref, far_ref, q_ref, wkv_ref, kv_in, heads_ref, kv, *, doms, per_dev
):
    _, share, par, _, dom = my_place()
    head = NODE_BLK
    rows, width = q_ref.shape
    write_kv(far_ref, wkv_ref, kv, 4 * per_dev)

    scale = math.log2(math.e) / math.sqrt(head)
    blocks = rows // NODE_BLK
    for b in range(blocks):
        row = share * blocks + b
        count = count_ref[row]
        where = []
        for j in range(KMAX):
            entry = list_ref[row, j]
            part = lax.div(entry, per_dev)
            step = lax.rem(part - dom + (doms + 2), doms) - 2
            turned = jnp.where(par == 0, step, -step)
            slot = jnp.where(
                turned >= 0, jnp.where(turned == 0, 0, turned), jnp.where(turned == -1, 3, 4)
            )
            where.append(slot * per_dev + lax.rem(entry, per_dev))
        at = slice(b * NODE_BLK, (b + 1) * NODE_BLK)
        for pair in range(HEADS // 2):
            col = pair * 4 * head
            keys = jnp.concatenate([kv[i, :, col : col + 2 * head] for i in where], axis=0)
            vals = jnp.concatenate(
                [kv[i, :, col + 2 * head : col + 4 * head] for i in where], axis=0
            )
            q0 = q_ref[at, 2 * pair * head : (2 * pair + 1) * head]
            q1 = q_ref[at, (2 * pair + 1) * head : (2 * pair + 2) * head]
            zero = jnp.zeros_like(q0)
            query = jnp.concatenate(
                [jnp.concatenate([q0, zero], axis=1), jnp.concatenate([zero, q1], axis=1)], axis=0
            )
            scores = lax.dot_general(
                query, keys, (((1,), (1,)), ((), ())), preferred_element_type=jnp.float32
            )
            parts = [
                jnp.where(j < count, scores[:, j * NODE_BLK : (j + 1) * NODE_BLK], -1e30)
                for j in range(KMAX)
            ]
            top = jnp.max(functools.reduce(jnp.maximum, parts), axis=-1, keepdims=True)
            parts = [jnp.exp2((p - top) * scale) for p in parts]
            total = jnp.sum(functools.reduce(jnp.add, parts), axis=-1, keepdims=True)
            mixed = matmul(jnp.concatenate([bf(p) for p in parts], axis=1), vals) / total
            heads_ref[at, 2 * pair * head : (2 * pair + 1) * head] = bf(mixed[:head, :head])
            heads_ref[at, (2 * pair + 1) * head : (2 * pair + 2) * head] = bf(mixed[head:, head:])


def attend(listed, counts, far, query, wkv, kv, per_dev, doms):
    rows, width = query.shape
    return pl.pallas_call(
        functools.partial(attend_kernel, doms=doms, per_dev=per_dev),
        in_specs=[SMEM] * 2 + [VMEM] * 4,
        out_specs=[VMEM] * 2,
        out_shape=[in_vmem((rows, width)), in_vmem(kv.shape)],
        input_output_aliases={5: 1},
        name="attend",
        compiler_params=pltpu.CompilerParams(vmem_limit_bytes=16 * MIB),
        cost_estimate=cost(
            4 * rows * width * KMAX * NODE_BLK + 4 * rows * width**2,
            10 * MIB,
            rows * HEADS * KMAX * NODE_BLK,
        ),
    )(listed, counts, far, query, wkv, kv)[0]


def mlp_kernel(
    heads_ref, gain_ref, shift_ref, out_w, up_w, down_w, p1, p1s, p2, p2s, state_ref,
    o0, o1, o2, o3,
    rows_in, last, resid_ref, hidden_ref, sem,
):
    sample, share, par, rank, _ = my_place()
    head = NODE_BLK
    rows, width = heads_ref.shape
    copy = pltpu.make_async_copy(state_ref.at[sample, aligned(share, rows)], rows_in, sem)
    copy.start()
    half = p2.shape[0]
    last[aligned(par, half)] = p2[...]
    last[aligned(1 - par, half)] = p2s[...]
    packs = (p1, p1s, last)
    out_all = jnp.concatenate([out_w[...]] + [p[width : width + head] for p in packs], axis=0)
    mixed = matmul(heads_ref[...], out_all)
    copy.wait()
    resid_ref[...] = rows_in[...].astype(jnp.float32) + mixed
    s = pl.ds(sample, 1)
    normed = bf(normalise(resid_ref[...], gain_ref[1, s], shift_ref[1, s]))
    for h in range(HEADS):
        v = matmul(normed, up_w[...] if h == 0 else packs[h - 1][:width])
        hidden_ref[:, h * width : (h + 1) * width] = bf(0.5 * v * (1.0 + jnp.tanh(0.5 * v)))
    down_all = jnp.concatenate([down_w[...]] + [p[width + head :] for p in packs], axis=0)
    resid_ref[...] += matmul(hidden_ref[...], down_all)
    for r, o_ref in enumerate((o0, o1, o2, o3)):
        o_ref[...] = bf(resid_ref[:, aligned(lax.rem(rank + r, HEADS), head)])


def mlp(heads, gain, shift, weights, state):
    rows, width = heads.shape
    head = NODE_BLK
    return pl.pallas_call(
        mlp_kernel,
        in_specs=[VMEM] * (3 + len(weights)) + [HBM],
        out_specs=[VMEM] * HEADS,
        out_shape=[shape((rows, head))] * HEADS,
        scratch_shapes=[
            pltpu.VMEM((rows, width), jnp.bfloat16),
            pltpu.VMEM((2 * width + head, width), jnp.bfloat16),
            pltpu.VMEM((rows, width), jnp.float32),
            pltpu.VMEM((rows, HEADS * width), jnp.bfloat16),
            pltpu.SemaphoreType.DMA,
        ],
        name="mlp",
        compiler_params=pltpu.CompilerParams(vmem_limit_bytes=24 * MIB),
        cost_estimate=cost(18 * rows * width * width, 8 * MIB, rows * HEADS * width),
    )(heads, gain, shift, *weights, kept_in_hbm(state))


def place_kernel(own, a, b, c, o_ref):
    rank = my_place()[3]
    for off, r in ((0, own), (3, a), (1, b), (2, c)):
        o_ref[lax.rem(rank + off, HEADS)] = r[...]


def placed_rows(pieces):
    rows, head = pieces[0].shape
    return pl.pallas_call(
        place_kernel,
        in_specs=[VMEM] * HEADS,
        out_specs=VMEM,
        out_shape=shape((HEADS, rows, head)),
        name="place_rows",
        compiler_params=pltpu.CompilerParams(vmem_limit_bytes=4 * MIB),
        cost_estimate=cost(0, 16 * rows * head),
    )(*pieces)


def after(value, *deps):
    return lax.optimization_barrier((value, *deps))[0]


def local(
    state, norm_gain, norm_shift, qkv_weight, out_weight, up_weight, down_weight, neighbours, counts
):
    samples, row_count, width = state.shape
    per_dev = row_count // NODE_BLK
    doms = lax.axis_size("dom")
    tps = lax.axis_size("tp")
    dom = lax.axis_index("dom")
    par = lax.rem(dom, 2)

    def hop(v, pairs):
        return lax.ppermute(v, "dom", pairs)

    def sign(i):
        return 1 if i % 2 == 0 else -1

    def swap(v):
        return hop(v, [(i ^ 1, i) for i in range(doms)])

    def near(v):
        return hop(v, [((i + 2 * sign(i)) % doms, i) for i in range(doms)])

    def far(v):
        return hop(v, [((i - 2 * sign(i)) % doms, i) for i in range(doms)])

    def ring(v):
        pairs = [
            (i * tps + (t - sign(i)) % tps, i * tps + t) for i in range(doms) for t in range(tps)
        ]
        return lax.ppermute(v, ("dom", "tp"), pairs)

    def up(v):
        return lax.ppermute(v, "tp", [(i, (i + 1) % tps) for i in range(tps)])

    def down(v):
        return lax.ppermute(v, "tp", [((i + 1) % tps, i) for i in range(tps)])

    def across(v):
        return lax.ppermute(v, "tp", [(i, (i + 2) % tps) for i in range(tps)])

    own = normed_rows(state, norm_gain, norm_shift)
    qkv = jnp.transpose(qkv_weight, (1, 0, 2))
    w1 = ring(after(qkv, own))
    near_rows = near(own)
    partner = swap(own)
    pack = packed(after(up_weight, own), out_weight, down_weight)

    w2 = swap(w1)
    mid = width // 2
    w3m = ring(lax.dynamic_slice_in_dim(w1, par * mid, mid, 1))
    w3t = swap(w3m)
    p1 = ring(after(pack, w3m))

    own_late, near_rows = lax.optimization_barrier((own, near_rows))
    far_rows = far(own_late)
    relay = swap(near_rows)
    kv, query, wkv = kv_first(own_late, partner, (qkv, w1, w2, w3m, w3t), 5)
    mid = pack.shape[0] // 2
    p1 = after(p1, query)
    p1s = swap(p1)
    p2 = ring(lax.dynamic_slice_in_dim(p1, par * mid, mid, 0))
    kv = kv_second(near_rows, relay, wkv, kv)
    p2, kv = lax.optimization_barrier((p2, kv))
    p2s = swap(p2)

    heads = attend(neighbours, counts, far_rows, query, wkv, kv, per_dev, doms)
    weights = (out_weight, up_weight, down_weight, p1, p1s, p2, p2s)
    mine = mlp(heads, norm_gain, norm_shift, weights, state)
    out = placed_rows((mine[0], up(mine[1]), down(mine[3]), across(mine[2])))
    return out.reshape(samples, row_count, width // tps)


def solution(mesh):
    placed = (
        P(None, "dom", None),
        P(),
        P(),
        P(None, None, "tp"),
        P("tp", None),
        P(None, "tp"),
        P("tp", None),
        P("dom", None),
        P("dom"),
    )
    return jax.shard_map(
        local, mesh=mesh, in_specs=placed, out_specs=P(None, "dom", "tp"), check_vma=False
    )
```

```python
import functools
import math

import jax
import jax.numpy as jnp
from jax import lax
from jax.experimental import pallas as pl
from jax.experimental.pallas import tpu as pltpu
from jax.sharding import PartitionSpec as P

HEADS = 4
NODE_BLK = 128
KMAX = 8
ROWS = 512
MIB = 1024 * 1024

VMEM = pl.BlockSpec(memory_space=pltpu.VMEM)
SMEM = pl.BlockSpec(memory_space=pltpu.SMEM)
HBM = pl.BlockSpec(memory_space=pltpu.HBM)


def bf(v):
    return v.astype(jnp.bfloat16)


def matmul(a, b):
    return jnp.dot(a, b, preferred_element_type=jnp.float32)


def aligned(i, step):
    return pl.ds(pl.multiple_of(i * step, step), step)


def shape(dims, dtype=jnp.bfloat16):
    return jax.ShapeDtypeStruct(dims, dtype)


def in_hbm(dims, dtype=jnp.bfloat16):
    return pltpu.HBM(dims, dtype)


def in_vmem(dims, dtype=jnp.bfloat16):
    return pltpu.VMEM(dims, dtype)


def kept_in_hbm(v):
    return pltpu.with_memory_space_constraint(v, pltpu.HBM)


def normalise(values, gain, shift):
    mean = jnp.mean(values, axis=-1, keepdims=True)
    centred = values - mean
    spread = jnp.mean(centred * centred, axis=-1, keepdims=True)
    return centred * lax.rsqrt(spread + 1e-05) * gain + shift


def my_place():
    dom = lax.axis_index("dom")
    rank = lax.axis_index("tp")
    return lax.div(rank, 2), lax.rem(rank, 2), lax.rem(dom, 2), rank, dom


def norm_kernel(state_ref, gain_ref, shift_ref, o_ref, x_in, affine, sems):
    sample = my_place()[0]
    s = pl.ds(sample, 1)
    chunks = sems.shape[0] - 2
    step = x_in.shape[0] // chunks
    spans = [pl.ds(k * step, step) for k in range(chunks)]
    loads = [
        pltpu.make_async_copy(state_ref.at[sample, at], x_in.at[at], sems.at[k])
        for k, at in enumerate(spans)
    ]
    small = [
        pltpu.make_async_copy(r, affine.at[k], sems.at[chunks + k])
        for k, r in enumerate((gain_ref, shift_ref))
    ]
    for c in loads[:1] + small + loads[1:]:
        c.start()
    for c in small:
        c.wait()
    gain, shift = affine[0, 0, s], affine[1, 0, s]
    for c, at in zip(loads, spans):
        c.wait()
        o_ref[at] = bf(normalise(x_in[at].astype(jnp.float32), gain, shift))


def normed_rows(state, gain, shift):
    _, rows, width = state.shape
    return pl.pallas_call(
        norm_kernel,
        in_specs=[HBM] * 3,
        out_specs=VMEM,
        out_shape=in_vmem((rows, width)),
        scratch_shapes=[
            pltpu.VMEM((rows, width), jnp.bfloat16),
            pltpu.VMEM((2, *gain.shape), jnp.float32),
            pltpu.SemaphoreType.DMA((6,)),
        ],
        name="norm_rows",
        compiler_params=pltpu.CompilerParams(vmem_limit_bytes=8 * MIB),
    )(kept_in_hbm(state), kept_in_hbm(gain), kept_in_hbm(shift))


def pack_kernel(qkv_ref, out_ref, o_ref):
    parts = qkv_ref.shape[0]
    head = NODE_BLK
    o_ref[:parts] = qkv_ref[...]
    for k in range(HEADS):
        o_ref[parts, k * head : (k + 1) * head] = out_ref[:, k * head : (k + 1) * head]


def packed(qkv, out_w):
    parts, width, head = qkv.shape
    return pl.pallas_call(
        pack_kernel,
        in_specs=[VMEM] * 2,
        out_specs=VMEM,
        out_shape=in_vmem((parts + 1, width, head)),
        name="pack_weights",
        compiler_params=pltpu.CompilerParams(vmem_limit_bytes=4 * MIB),
    )(qkv, out_w)


def relay_kernel(a_ref, b_ref, o_ref):
    par = my_place()[2]

    @pl.when(par == 0)
    def _():
        o_ref[...] = a_ref[...]

    @pl.when(par == 1)
    def _():
        o_ref[...] = b_ref[...]


def one_to_relay(a, b):
    return pl.pallas_call(
        relay_kernel,
        in_specs=[VMEM] * 2,
        out_specs=VMEM,
        out_shape=in_vmem(a.shape),
        name="one_to_relay",
        compiler_params=pltpu.CompilerParams(vmem_limit_bytes=4 * MIB),
    )(a, b)


def write_kv(x_ref, wkv_ref, kv_ref, first):
    rows, width = x_ref.shape
    for r in range(0, rows, ROWS):
        out = bf(matmul(x_ref[r : r + ROWS], wkv_ref[...]))
        at = first + r // NODE_BLK
        kv_ref[at : at + ROWS // NODE_BLK] = out.reshape((ROWS // NODE_BLK, NODE_BLK, 2 * width))


def kv_first_kernel(xa, xb, w0, w1, w2, w3m, w3t, kv_ref, q_ref, wkv_ref, wo_ref, wq_ref):
    head = NODE_BLK
    _, share, par, _, _ = my_place()
    half = w3m.shape[1]
    halves = ((par, w3m), (1 - par, w3t))
    for h in range(HEADS):
        at = (h // 2) * 4 * head + (h % 2) * head
        spots = ((0, wq_ref, h * head), (1, wkv_ref, at), (2, wkv_ref, at + 2 * head))
        for c, dst, col in spots:
            if h < 3:
                dst[:, col : col + head] = (w0, w1, w2)[h][c]
            else:
                for which, w in halves:
                    dst[aligned(which, half), col : col + head] = w[c]
        rows = slice(h * head, (h + 1) * head)
        if h < 3:
            for k in range(HEADS):
                wo_ref[rows, k * head : (k + 1) * head] = (w0, w1, w2)[h][3, k * head : (k + 1) * head]
        else:
            for which, w in halves:
                for k in range(HEADS // 2):
                    wo_ref[rows, aligned(which * (HEADS // 2) + k, head)] = w[
                        3, k * head : (k + 1) * head
                    ]
    write_kv(xa, wkv_ref, kv_ref, 0)
    write_kv(xb, wkv_ref, kv_ref, xa.shape[0] // NODE_BLK)
    q_ref[...] = bf(matmul(xa[aligned(share, q_ref.shape[0])], wq_ref[...]))


def kv_first(xa, xb, weights, slots):
    rows, width = xa.shape
    return pl.pallas_call(
        kv_first_kernel,
        in_specs=[VMEM] * (2 + len(weights)),
        out_specs=[VMEM] * 4,
        scratch_shapes=[pltpu.VMEM((width, width), jnp.bfloat16)],
        out_shape=[
            in_vmem((slots * rows // NODE_BLK, NODE_BLK, 2 * width)),
            in_vmem((rows // 2, width)),
            in_vmem((width, 2 * width)),
            in_vmem((width, width)),
        ],
        name="kv_first",
        compiler_params=pltpu.CompilerParams(vmem_limit_bytes=16 * MIB),
    )(xa, xb, *weights)


def kv_second_kernel(xa, xb, wkv_ref, kv_in, kv_ref):
    first = 2 * xa.shape[0] // NODE_BLK
    write_kv(xa, wkv_ref, kv_ref, first)
    write_kv(xb, wkv_ref, kv_ref, first + xa.shape[0] // NODE_BLK)


def kv_second(xa, xb, wkv, kv):
    rows, width = xa.shape
    return pl.pallas_call(
        kv_second_kernel,
        in_specs=[VMEM] * 4,
        out_specs=VMEM,
        out_shape=in_vmem(kv.shape),
        input_output_aliases={3: 0},
        name="kv_second",
        compiler_params=pltpu.CompilerParams(vmem_limit_bytes=16 * MIB),
    )(xa, xb, wkv, kv)


def attend_kernel(
    list_ref, count_ref, relay_ref, q_ref, wkv_ref, kv_in, heads_ref, kv, *, doms, per_dev
):
    _, share, par, _, dom = my_place()
    head = NODE_BLK
    rows, width = q_ref.shape
    write_kv(relay_ref, wkv_ref, kv, 4 * per_dev)

    scale = math.log2(math.e) / math.sqrt(head)
    blocks = rows // NODE_BLK
    for b in range(blocks):
        row = share * blocks + b
        count = count_ref[row]
        where = []
        for j in range(KMAX):
            entry = list_ref[row, j]
            part = lax.div(entry, per_dev)
            step = lax.rem(part - dom + (doms + 2), doms) - 2
            turned = jnp.where(par == 0, step, -step)
            slot = jnp.where(turned >= 0, turned, turned + 5)
            where.append(slot * per_dev + lax.rem(entry, per_dev))
        at = slice(b * NODE_BLK, (b + 1) * NODE_BLK)
        for pair in range(HEADS // 2):
            col = pair * 4 * head
            keys = jnp.concatenate([kv[i, :, col : col + 2 * head] for i in where], axis=0)
            vals = jnp.concatenate(
                [kv[i, :, col + 2 * head : col + 4 * head] for i in where], axis=0
            )
            q0 = q_ref[at, 2 * pair * head : (2 * pair + 1) * head]
            q1 = q_ref[at, (2 * pair + 1) * head : (2 * pair + 2) * head]
            zero = jnp.zeros_like(q0)
            query = jnp.concatenate(
                [jnp.concatenate([q0, zero], axis=1), jnp.concatenate([zero, q1], axis=1)], axis=0
            )
            scores = lax.dot_general(
                query, keys, (((1,), (1,)), ((), ())), preferred_element_type=jnp.float32
            )
            parts = [
                jnp.where(j < count, scores[:, j * NODE_BLK : (j + 1) * NODE_BLK], -1e30)
                for j in range(KMAX)
            ]
            top = jnp.max(functools.reduce(jnp.maximum, parts), axis=-1, keepdims=True)
            parts = [jnp.exp2((p - top) * scale) for p in parts]
            total = jnp.sum(functools.reduce(jnp.add, parts), axis=-1, keepdims=True)
            mixed = matmul(jnp.concatenate([bf(p) for p in parts], axis=1), vals) / total
            heads_ref[at, 2 * pair * head : (2 * pair + 1) * head] = bf(mixed[:head, :head])
            heads_ref[at, (2 * pair + 1) * head : (2 * pair + 2) * head] = bf(mixed[head:, head:])


def attend(listed, counts, relay, query, wkv, kv, per_dev, doms):
    rows, width = query.shape
    return pl.pallas_call(
        functools.partial(attend_kernel, doms=doms, per_dev=per_dev),
        in_specs=[SMEM] * 2 + [VMEM] * 4,
        out_specs=[VMEM] * 2,
        out_shape=[in_vmem((rows, width)), in_vmem(kv.shape)],
        input_output_aliases={5: 1},
        name="attend",
        compiler_params=pltpu.CompilerParams(vmem_limit_bytes=16 * MIB),
    )(listed, counts, relay, query, wkv, kv)[0]


def silu(v):
    return 0.5 * v * (1.0 + jnp.tanh(0.5 * v))


def mlp_first_kernel(
    heads_ref, gain_ref, shift_ref, wo_ref, u0, d0, u1, d1, u2, d2, state_ref,
    resid_ref, normed_ref,
    rows_in, hidden_ref, sem,
):
    sample, share, _, _, _ = my_place()
    rows, width = heads_ref.shape
    copy = pltpu.make_async_copy(state_ref.at[sample, aligned(share, rows)], rows_in, sem)
    copy.start()
    mixed = matmul(heads_ref[...], wo_ref[...])
    copy.wait()
    resid_ref[...] = rows_in[...].astype(jnp.float32) + mixed
    s = pl.ds(sample, 1)
    normed_ref[...] = bf(normalise(resid_ref[...], gain_ref[1, s], shift_ref[1, s]))
    for k, u in enumerate((u0, u1, u2)):
        hidden_ref[:, k * width : (k + 1) * width] = bf(silu(matmul(normed_ref[...], u[...])))
    downs = jnp.concatenate([d0[...], d1[...], d2[...]], axis=0)
    resid_ref[...] += matmul(hidden_ref[...], downs)


def mlp_first(heads, gain, shift, wo, weights, state):
    rows, width = heads.shape
    return pl.pallas_call(
        mlp_first_kernel,
        in_specs=[VMEM] * (4 + len(weights)) + [HBM],
        out_specs=[VMEM] * 2,
        out_shape=[in_vmem((rows, width), jnp.float32), in_vmem((rows, width))],
        scratch_shapes=[
            pltpu.VMEM((rows, width), jnp.bfloat16),
            pltpu.VMEM((rows, 3 * width), jnp.bfloat16),
            pltpu.SemaphoreType.DMA,
        ],
        name="mlp_first",
        compiler_params=pltpu.CompilerParams(vmem_limit_bytes=16 * MIB),
    )(heads, gain, shift, wo, *weights, kept_in_hbm(state))


def mlp_second_kernel(resid_ref, normed_ref, mine, theirs, o0, o1, o2, o3, total_ref, up_ref, down_ref):
    _, _, par, rank, _ = my_place()
    head = NODE_BLK

    @pl.when(par == 0)
    def _():
        up_ref[...] = mine[...]
        down_ref[...] = theirs[...]

    @pl.when(par == 1)
    def _():
        up_ref[...] = theirs[...]
        down_ref[...] = mine[...]

    hidden = bf(silu(matmul(normed_ref[...], up_ref[...])))
    total_ref[...] = resid_ref[...] + matmul(hidden, down_ref[...])
    for r, o_ref in enumerate((o0, o1, o2, o3)):
        o_ref[...] = bf(total_ref[:, aligned(lax.rem(rank + r, HEADS), head)])


def mlp_second(resid, normed, mine, theirs):
    rows, width = normed.shape
    return pl.pallas_call(
        mlp_second_kernel,
        in_specs=[VMEM] * 4,
        out_specs=[VMEM] * HEADS,
        out_shape=[in_vmem((rows, width // HEADS))] * HEADS,
        scratch_shapes=[
            pltpu.VMEM((rows, width), jnp.float32),
            pltpu.VMEM(mine.shape, jnp.bfloat16),
            pltpu.VMEM(mine.shape, jnp.bfloat16),
        ],
        name="mlp_second",
        compiler_params=pltpu.CompilerParams(vmem_limit_bytes=16 * MIB),
    )(resid, normed, mine, theirs)


def place_kernel(own, a, b, c, o_ref):
    rank = my_place()[3]
    for off, r in ((0, own), (3, a), (1, b), (2, c)):
        o_ref[lax.rem(rank + off, HEADS)] = r[...]


def placed_rows(pieces):
    rows, head = pieces[0].shape
    return pl.pallas_call(
        place_kernel,
        in_specs=[VMEM] * HEADS,
        out_specs=VMEM,
        out_shape=shape((HEADS, rows, head)),
        name="place_rows",
        compiler_params=pltpu.CompilerParams(vmem_limit_bytes=4 * MIB),
    )(*pieces)


def after(value, *deps):
    return lax.optimization_barrier((value, *deps))[0]


def local(
    state, norm_gain, norm_shift, qkv_weight, out_weight, up_weight, down_weight, neighbours, counts
):
    samples, row_count, width = state.shape
    per_dev = row_count // NODE_BLK
    doms = lax.axis_size("dom")
    tps = lax.axis_size("tp")
    dom = lax.axis_index("dom")
    par = lax.rem(dom, 2)

    def hop(v, pairs):
        return lax.ppermute(v, "dom", pairs)

    def sign(i):
        return 1 if i % 2 == 0 else -1

    def swap(v):
        return hop(v, [(i ^ 1, i) for i in range(doms)])

    def near(v):
        return hop(v, [((i + 2 * sign(i)) % doms, i) for i in range(doms)])

    def far(v):
        return hop(v, [((i - 2 * sign(i)) % doms, i) for i in range(doms)])

    def ring(v):
        pairs = [
            (i * tps + (t - sign(i)) % tps, i * tps + t) for i in range(doms) for t in range(tps)
        ]
        return lax.ppermute(v, ("dom", "tp"), pairs)

    def up(v):
        return lax.ppermute(v, "tp", [(i, (i + 1) % tps) for i in range(tps)])

    def down(v):
        return lax.ppermute(v, "tp", [((i + 1) % tps, i) for i in range(tps)])

    def across(v):
        return lax.ppermute(v, "tp", [(i, (i + 2) % tps) for i in range(tps)])

    w0 = packed(jnp.transpose(qkv_weight, (1, 0, 2)), out_weight)
    w1 = ring(w0)
    own = normed_rows(after(state, w0), norm_gain, norm_shift)
    partner = swap(own)
    near_rows, far_rows = near(own), far(own)

    w1 = after(w1, partner)
    w2 = swap(w1)
    mid = width // 2
    w1_half = lax.dynamic_slice_in_dim(w1, par * mid, mid, 1)
    w3m = ring(w1_half)
    w3t = swap(w3m)
    up_late, down_late, w1_half = lax.optimization_barrier((up_weight, down_weight, w1_half))
    u1, d1 = ring(up_late), ring(down_late)

    kv, query, wkv, wo = kv_first(own, partner, (w0, w1, w2, w3m, w3t), 5)
    near_rows, far_rows, query = lax.optimization_barrier((near_rows, far_rows, query))
    relay = swap(near_rows)
    u1, d1 = lax.optimization_barrier((u1, d1, query))[:2]
    u2, d2 = swap(u1), swap(d1)
    last = ring(one_to_relay(u1, d1))
    kv = kv_second(near_rows, far_rows, wkv, kv)

    heads = attend(neighbours, counts, relay, query, wkv, kv, per_dev, doms)
    last, heads = lax.optimization_barrier((last, heads))
    last_too = swap(last)
    weights = (up_weight, down_weight, u1, d1, u2, d2)
    resid, normed = mlp_first(heads, norm_gain, norm_shift, wo, weights, state)
    mine = mlp_second(resid, normed, last, last_too)
    out = placed_rows((mine[0], up(mine[1]), down(mine[3]), across(mine[2])))
    return out.reshape(samples, row_count, width // tps)


def solution(mesh):
    placed = (
        P(None, "dom", None),
        P(),
        P(),
        P(None, None, "tp"),
        P("tp", None),
        P(None, "tp"),
        P("tp", None),
        P("dom", None),
        P("dom"),
    )
    return jax.shard_map(
        local, mesh=mesh, in_specs=placed, out_specs=P(None, "dom", "tp"), check_vma=False
    )
```

```python
import functools
import math

import jax
import jax.numpy as jnp
from jax import lax
from jax.experimental import pallas as pl
from jax.experimental.pallas import tpu as pltpu
from jax.sharding import PartitionSpec as P

HEADS = 4
NODE_BLK = 128
KMAX = 8
ROWS = 512
MIB = 1024 * 1024

VMEM = pl.BlockSpec(memory_space=pltpu.VMEM)
SMEM = pl.BlockSpec(memory_space=pltpu.SMEM)
HBM = pl.BlockSpec(memory_space=pltpu.HBM)


def bf(v):
    return v.astype(jnp.bfloat16)


def matmul(a, b):
    return jnp.dot(a, b, preferred_element_type=jnp.float32)


def aligned(i, step):
    return pl.ds(pl.multiple_of(i * step, step), step)


def shape(dims, dtype=jnp.bfloat16):
    return jax.ShapeDtypeStruct(dims, dtype)


def in_hbm(dims, dtype=jnp.bfloat16):
    return pltpu.HBM(dims, dtype)


def in_vmem(dims, dtype=jnp.bfloat16):
    return pltpu.VMEM(dims, dtype)


def kept_in_hbm(v):
    return pltpu.with_memory_space_constraint(v, pltpu.HBM)


def normalise(values, gain, shift):
    mean = jnp.mean(values, axis=-1, keepdims=True)
    centred = values - mean
    spread = jnp.mean(centred * centred, axis=-1, keepdims=True)
    return centred * lax.rsqrt(spread + 1e-05) * gain + shift


def my_place():
    dom = lax.axis_index("dom")
    rank = lax.axis_index("tp")
    return lax.div(rank, 2), lax.rem(rank, 2), lax.rem(dom, 2), rank, dom


def prepare_kernel(
    state_ref, gain_ref, shift_ref, qkv_ref, out_ref, o_ref, w_ref, x_in, affine, sems
):
    sample = my_place()[0]
    s = pl.ds(sample, 1)
    head = NODE_BLK
    chunks = 4
    step = x_in.shape[0] // chunks
    parts = qkv_ref.shape[0]
    spans = [pl.ds(k * step, step) for k in range(chunks)]
    jobs = [(state_ref.at[sample, at], x_in.at[at]) for at in spans]
    jobs += [(gain_ref, affine.at[0]), (shift_ref, affine.at[1]), (qkv_ref, w_ref.at[pl.ds(0, parts)])]
    jobs += [
        (out_ref.at[:, pl.ds(k * head, head)], w_ref.at[parts, pl.ds(k * head, head)])
        for k in range(HEADS)
    ]
    copies = [pltpu.make_async_copy(a, b, sems.at[k]) for k, (a, b) in enumerate(jobs)]
    for k in (0, chunks, chunks + 1, *range(1, chunks), *range(chunks + 2, len(jobs))):
        copies[k].start()
    for c in copies[chunks : chunks + 2]:
        c.wait()
    gain, shift = affine[0, 0, s], affine[1, 0, s]
    for c, at in zip(copies, spans):
        c.wait()
        o_ref[at] = bf(normalise(x_in[at].astype(jnp.float32), gain, shift))
    for c in copies[chunks + 2 :]:
        c.wait()


def prepare(state, gain, shift, qkv, out_w):
    _, rows, width = state.shape
    parts, _, head = qkv.shape
    return pl.pallas_call(
        prepare_kernel,
        in_specs=[HBM] * 5,
        out_specs=[VMEM] * 2,
        out_shape=[in_vmem((rows, width)), in_vmem((parts + 1, width, head))],
        scratch_shapes=[
            pltpu.VMEM((rows, width), jnp.bfloat16),
            pltpu.VMEM((2, *gain.shape), jnp.float32),
            pltpu.SemaphoreType.DMA((7 + HEADS,)),
        ],
        name="prepare",
        compiler_params=pltpu.CompilerParams(vmem_limit_bytes=6 * MIB),
    )(*[kept_in_hbm(v) for v in (state, gain, shift, qkv, out_w)])


def relay_kernel(a_ref, b_ref, o_ref):
    par = my_place()[2]

    @pl.when(par == 0)
    def _():
        o_ref[...] = a_ref[...]

    @pl.when(par == 1)
    def _():
        o_ref[...] = b_ref[...]


def one_to_relay(a, b):
    return pl.pallas_call(
        relay_kernel,
        in_specs=[VMEM] * 2,
        out_specs=VMEM,
        out_shape=in_vmem(a.shape),
        name="one_to_relay",
        compiler_params=pltpu.CompilerParams(vmem_limit_bytes=4 * MIB),
    )(a, b)


def write_kv(x_ref, wkv_ref, kv_ref, first):
    rows, width = x_ref.shape
    for r in range(0, rows, ROWS):
        out = bf(matmul(x_ref[r : r + ROWS], wkv_ref[...]))
        at = first + r // NODE_BLK
        kv_ref[at : at + ROWS // NODE_BLK] = out.reshape((ROWS // NODE_BLK, NODE_BLK, 2 * width))


def kv_first_kernel(xa, xb, w0, w1, w2, w3m, w3t, kv_ref, q_ref, wkv_ref, wo_ref, wq_ref):
    head = NODE_BLK
    _, share, par, _, _ = my_place()
    half = w3m.shape[1]
    halves = ((par, w3m), (1 - par, w3t))
    for h in range(HEADS):
        at = (h // 2) * 4 * head + (h % 2) * head
        spots = ((0, wq_ref, h * head), (1, wkv_ref, at), (2, wkv_ref, at + 2 * head))
        for c, dst, col in spots:
            if h < 3:
                dst[:, col : col + head] = (w0, w1, w2)[h][c]
            else:
                for which, w in halves:
                    dst[aligned(which, half), col : col + head] = w[c]
        rows = slice(h * head, (h + 1) * head)
        if h < 3:
            for k in range(HEADS):
                wo_ref[rows, k * head : (k + 1) * head] = (w0, w1, w2)[h][3, k * head : (k + 1) * head]
        else:
            for which, w in halves:
                for k in range(HEADS // 2):
                    wo_ref[rows, aligned(which * (HEADS // 2) + k, head)] = w[
                        3, k * head : (k + 1) * head
                    ]
    write_kv(xa, wkv_ref, kv_ref, 0)
    write_kv(xb, wkv_ref, kv_ref, xa.shape[0] // NODE_BLK)
    q_ref[...] = bf(matmul(xa[aligned(share, q_ref.shape[0])], wq_ref[...]))


def kv_first(xa, xb, weights, slots):
    rows, width = xa.shape
    return pl.pallas_call(
        kv_first_kernel,
        in_specs=[VMEM] * (2 + len(weights)),
        out_specs=[VMEM] * 4,
        scratch_shapes=[pltpu.VMEM((width, width), jnp.bfloat16)],
        out_shape=[
            in_vmem((slots * rows // NODE_BLK, NODE_BLK, 2 * width)),
            in_vmem((rows // 2, width)),
            in_vmem((width, 2 * width)),
            in_vmem((width, width)),
        ],
        name="kv_first",
        compiler_params=pltpu.CompilerParams(vmem_limit_bytes=12 * MIB),
    )(xa, xb, *weights)


def kv_second_kernel(xa, xb, wkv_ref, kv_in, kv_ref):
    first = 2 * xa.shape[0] // NODE_BLK
    write_kv(xa, wkv_ref, kv_ref, first)
    write_kv(xb, wkv_ref, kv_ref, first + xa.shape[0] // NODE_BLK)


def kv_second(xa, xb, wkv, kv):
    rows, width = xa.shape
    return pl.pallas_call(
        kv_second_kernel,
        in_specs=[VMEM] * 4,
        out_specs=VMEM,
        out_shape=in_vmem(kv.shape),
        input_output_aliases={3: 0},
        name="kv_second",
        compiler_params=pltpu.CompilerParams(vmem_limit_bytes=12 * MIB),
    )(xa, xb, wkv, kv)


def attend_kernel(
    list_ref, count_ref, relay_ref, q_ref, wkv_ref, kv_in, heads_ref, kv, *, doms, per_dev
):
    _, share, par, _, dom = my_place()
    head = NODE_BLK
    rows, width = q_ref.shape
    write_kv(relay_ref, wkv_ref, kv, 4 * per_dev)

    scale = math.log2(math.e) / math.sqrt(head)
    blocks = rows // NODE_BLK
    for b in range(blocks):
        row = share * blocks + b
        count = count_ref[row]
        where = []
        for j in range(KMAX):
            entry = list_ref[row, j]
            part = lax.div(entry, per_dev)
            step = lax.rem(part - dom + (doms + 2), doms) - 2
            turned = jnp.where(par == 0, step, -step)
            slot = jnp.where(turned >= 0, turned, turned + 5)
            where.append(slot * per_dev + lax.rem(entry, per_dev))
        at = slice(b * NODE_BLK, (b + 1) * NODE_BLK)
        for pair in range(HEADS // 2):
            col = pair * 4 * head
            keys = jnp.concatenate([kv[i, :, col : col + 2 * head] for i in where], axis=0)
            vals = jnp.concatenate(
                [kv[i, :, col + 2 * head : col + 4 * head] for i in where], axis=0
            )
            q0 = q_ref[at, 2 * pair * head : (2 * pair + 1) * head]
            q1 = q_ref[at, (2 * pair + 1) * head : (2 * pair + 2) * head]
            zero = jnp.zeros_like(q0)
            query = jnp.concatenate(
                [jnp.concatenate([q0, zero], axis=1), jnp.concatenate([zero, q1], axis=1)], axis=0
            )
            scores = lax.dot_general(
                query, keys, (((1,), (1,)), ((), ())), preferred_element_type=jnp.float32
            )
            parts = [
                jnp.where(j < count, scores[:, j * NODE_BLK : (j + 1) * NODE_BLK], -1e30)
                for j in range(KMAX)
            ]
            top = jnp.max(functools.reduce(jnp.maximum, parts), axis=-1, keepdims=True)
            parts = [jnp.exp2((p - top) * scale) for p in parts]
            total = jnp.sum(functools.reduce(jnp.add, parts), axis=-1, keepdims=True)
            mixed = matmul(jnp.concatenate([bf(p) for p in parts], axis=1), vals) / total
            heads_ref[at, 2 * pair * head : (2 * pair + 1) * head] = bf(mixed[:head, :head])
            heads_ref[at, (2 * pair + 1) * head : (2 * pair + 2) * head] = bf(mixed[head:, head:])


def attend(listed, counts, relay, query, wkv, kv, per_dev, doms):
    rows, width = query.shape
    return pl.pallas_call(
        functools.partial(attend_kernel, doms=doms, per_dev=per_dev),
        in_specs=[SMEM] * 2 + [VMEM] * 4,
        out_specs=[VMEM] * 2,
        out_shape=[in_vmem((rows, width)), in_vmem(kv.shape)],
        input_output_aliases={5: 1},
        name="attend",
        compiler_params=pltpu.CompilerParams(vmem_limit_bytes=12 * MIB),
    )(listed, counts, relay, query, wkv, kv)[0]


def silu(v):
    return 0.5 * v * (1.0 + jnp.tanh(0.5 * v))


def mlp_first_kernel(
    heads_ref, gain_ref, shift_ref, wo_ref, u0, d0, u1, d1, u2, d2, state_ref,
    resid_ref, normed_ref,
    rows_in, hidden_ref, sem,
):
    sample, share, _, _, _ = my_place()
    rows, width = heads_ref.shape
    copy = pltpu.make_async_copy(state_ref.at[sample, aligned(share, rows)], rows_in, sem)
    copy.start()
    mixed = matmul(heads_ref[...], wo_ref[...])
    copy.wait()
    resid_ref[...] = rows_in[...].astype(jnp.float32) + mixed
    s = pl.ds(sample, 1)
    normed_ref[...] = bf(normalise(resid_ref[...], gain_ref[1, s], shift_ref[1, s]))
    for k, u in enumerate((u0, u1, u2)):
        hidden_ref[:, k * width : (k + 1) * width] = bf(silu(matmul(normed_ref[...], u[...])))
    downs = jnp.concatenate([d0[...], d1[...], d2[...]], axis=0)
    resid_ref[...] += matmul(hidden_ref[...], downs)


def mlp_first(heads, gain, shift, wo, weights, state):
    rows, width = heads.shape
    return pl.pallas_call(
        mlp_first_kernel,
        in_specs=[VMEM] * (4 + len(weights)) + [HBM],
        out_specs=[VMEM] * 2,
        out_shape=[in_vmem((rows, width), jnp.float32), in_vmem((rows, width))],
        scratch_shapes=[
            pltpu.VMEM((rows, width), jnp.bfloat16),
            pltpu.VMEM((rows, 3 * width), jnp.bfloat16),
            pltpu.SemaphoreType.DMA,
        ],
        name="mlp_first",
        compiler_params=pltpu.CompilerParams(vmem_limit_bytes=12 * MIB),
    )(heads, gain, shift, wo, *weights, kept_in_hbm(state))


def mlp_second_kernel(resid_ref, normed_ref, mine, theirs, o0, o1, o2, o3, total_ref, up_ref, down_ref):
    _, _, par, rank, _ = my_place()
    head = NODE_BLK

    @pl.when(par == 0)
    def _():
        up_ref[...] = mine[...]
        down_ref[...] = theirs[...]

    @pl.when(par == 1)
    def _():
        up_ref[...] = theirs[...]
        down_ref[...] = mine[...]

    hidden = bf(silu(matmul(normed_ref[...], up_ref[...])))
    total_ref[...] = resid_ref[...] + matmul(hidden, down_ref[...])
    for r, o_ref in enumerate((o0, o1, o2, o3)):
        o_ref[...] = bf(total_ref[:, aligned(lax.rem(rank + r, HEADS), head)])


def mlp_second(resid, normed, mine, theirs):
    rows, width = normed.shape
    return pl.pallas_call(
        mlp_second_kernel,
        in_specs=[VMEM] * 4,
        out_specs=[VMEM] * HEADS,
        out_shape=[in_vmem((rows, width // HEADS))] * HEADS,
        scratch_shapes=[
            pltpu.VMEM((rows, width), jnp.float32),
            pltpu.VMEM(mine.shape, jnp.bfloat16),
            pltpu.VMEM(mine.shape, jnp.bfloat16),
        ],
        name="mlp_second",
        compiler_params=pltpu.CompilerParams(vmem_limit_bytes=12 * MIB),
    )(resid, normed, mine, theirs)


def place_kernel(own, across, after, before, o_ref):
    rank = my_place()[3]
    for off, r in ((0, own), (2, across), (1, after), (3, before)):
        o_ref[lax.rem(rank + off, HEADS)] = r[...]


def placed_rows(pieces):
    rows, head = pieces[0].shape
    return pl.pallas_call(
        place_kernel,
        in_specs=[VMEM] * HEADS,
        out_specs=VMEM,
        out_shape=shape((HEADS, rows, head)),
        name="place_rows",
        compiler_params=pltpu.CompilerParams(vmem_limit_bytes=4 * MIB),
    )(*pieces)


def after(value, *deps):
    return lax.optimization_barrier((value, *deps))[0]


def local(
    state, norm_gain, norm_shift, qkv_weight, out_weight, up_weight, down_weight, neighbours, counts
):
    samples, row_count, width = state.shape
    per_dev = row_count // NODE_BLK
    doms = lax.axis_size("dom")
    tps = lax.axis_size("tp")
    dom = lax.axis_index("dom")
    par = lax.rem(dom, 2)

    def hop(v, pairs):
        return lax.ppermute(v, "dom", pairs)

    def sign(i):
        return 1 if i % 2 == 0 else -1

    def swap(v):
        return hop(v, [(i ^ 1, i) for i in range(doms)])

    def near(v):
        return hop(v, [((i + 2 * sign(i)) % doms, i) for i in range(doms)])

    def far(v):
        return hop(v, [((i - 2 * sign(i)) % doms, i) for i in range(doms)])

    def ring(v):
        pairs = [
            (i * tps + (t - sign(i)) % tps, i * tps + t) for i in range(doms) for t in range(tps)
        ]
        return lax.ppermute(v, ("dom", "tp"), pairs)

    def up(v):
        return lax.ppermute(v, "tp", [(i, (i + 1) % tps) for i in range(tps)])

    def down(v):
        return lax.ppermute(v, "tp", [((i + 1) % tps, i) for i in range(tps)])

    def across(v):
        return lax.ppermute(v, "tp", [(i, (i + 2) % tps) for i in range(tps)])

    qkv = jnp.transpose(qkv_weight, (1, 0, 2))
    own, w0 = prepare(state, norm_gain, norm_shift, qkv, out_weight)
    w1 = ring(w0)
    partner = swap(own)
    near_rows, far_rows = near(own), far(own)
    u1 = ring(after(up_weight, own))

    w1 = after(w1, partner)
    w2 = swap(w1)
    mid = width // 2
    w1_half = lax.dynamic_slice_in_dim(w1, par * mid, mid, 1)
    w3m = ring(w1_half)
    w3t = swap(w3m)
    d1 = ring(after(down_weight, w3m))

    own_late, u1 = lax.optimization_barrier((own, u1))
    kv, query, wkv, wo = kv_first(own_late, partner, (w0, w1, w2, w3m, w3t), 5)
    relayed = one_to_relay(u1, d1)
    near_rows, far_rows, query, relayed = lax.optimization_barrier(
        (near_rows, far_rows, query, relayed)
    )
    last = ring(relayed)
    relay = swap(near_rows)
    kv = kv_second(near_rows, far_rows, wkv, kv)
    u2, d2 = swap(u1), swap(d1)

    heads = attend(neighbours, counts, relay, query, wkv, kv, per_dev, doms)
    last, heads = lax.optimization_barrier((last, heads))
    last_too = swap(last)
    weights = (up_weight, down_weight, u1, d1, u2, d2)
    resid, normed = mlp_first(heads, norm_gain, norm_shift, wo, weights, state)
    mine = mlp_second(resid, normed, last, last_too)
    out = placed_rows((mine[0], across(mine[2]), down(mine[3]), up(mine[1])))
    return out.reshape(samples, row_count, width // tps)


def solution(mesh):
    placed = (
        P(None, "dom", None),
        P(),
        P(),
        P(None, None, "tp"),
        P("tp", None),
        P(None, "tp"),
        P("tp", None),
        P("dom", None),
        P("dom"),
    )
    return jax.shard_map(
        local, mesh=mesh, in_specs=placed, out_specs=P(None, "dom", "tp"), check_vma=False
    )
```

```python
import functools
import math

import jax
import jax.numpy as jnp
from jax import lax
from jax.experimental import pallas as pl
from jax.experimental.pallas import tpu as pltpu
from jax.sharding import PartitionSpec as P

HEADS = 4
NODE_BLK = 128
KMAX = 8
ROWS = 512
MIB = 1024 * 1024

VMEM = pl.BlockSpec(memory_space=pltpu.VMEM)
SMEM = pl.BlockSpec(memory_space=pltpu.SMEM)
HBM = pl.BlockSpec(memory_space=pltpu.HBM)


def bf(v):
    return v.astype(jnp.bfloat16)


def matmul(a, b):
    return jnp.dot(a, b, preferred_element_type=jnp.float32)


def aligned(i, step):
    return pl.ds(pl.multiple_of(i * step, step), step)


def shape(dims, dtype=jnp.bfloat16):
    return jax.ShapeDtypeStruct(dims, dtype)


def in_hbm(dims, dtype=jnp.bfloat16):
    return pltpu.HBM(dims, dtype)


def in_vmem(dims, dtype=jnp.bfloat16):
    return pltpu.VMEM(dims, dtype)


def kept_in_hbm(v):
    return pltpu.with_memory_space_constraint(v, pltpu.HBM)


def normalise(values, gain, shift):
    mean = jnp.mean(values, axis=-1, keepdims=True)
    centred = values - mean
    spread = jnp.mean(centred * centred, axis=-1, keepdims=True)
    return centred * lax.rsqrt(spread + 1e-05) * gain + shift


def my_place():
    dom = lax.axis_index("dom")
    rank = lax.axis_index("tp")
    return lax.div(rank, 2), lax.rem(rank, 2), lax.rem(dom, 2), rank, dom


def norm_kernel(state_ref, gain_ref, shift_ref, o_ref, x_in, affine, sems):
    sample = my_place()[0]
    s = pl.ds(sample, 1)
    chunks = 4
    step = x_in.shape[0] // chunks
    spans = [pl.ds(k * step, step) for k in range(chunks)]
    jobs = [(state_ref.at[sample, at], x_in.at[at]) for at in spans]
    jobs += [(gain_ref, affine.at[0]), (shift_ref, affine.at[1])]
    copies = [pltpu.make_async_copy(a, b, sems.at[k]) for k, (a, b) in enumerate(jobs)]
    for k in (0, chunks, chunks + 1, *range(1, chunks)):
        copies[k].start()
    for c in copies[chunks:]:
        c.wait()
    gain, shift = affine[0, 0, s], affine[1, 0, s]
    for c, at in zip(copies, spans):
        c.wait()
        o_ref[at] = bf(normalise(x_in[at].astype(jnp.float32), gain, shift))


def normed_rows(state, gain, shift):
    _, rows, width = state.shape
    return pl.pallas_call(
        norm_kernel,
        in_specs=[HBM] * 3,
        out_specs=VMEM,
        out_shape=in_vmem((rows, width)),
        scratch_shapes=[
            pltpu.VMEM((rows, width), jnp.bfloat16),
            pltpu.VMEM((2, *gain.shape), jnp.float32),
            pltpu.SemaphoreType.DMA((6,)),
        ],
        name="norm_rows",
        compiler_params=pltpu.CompilerParams(vmem_limit_bytes=6 * MIB),
    )(*[kept_in_hbm(v) for v in (state, gain, shift)])


def pack_kernel(qkv_ref, out_ref, w_ref, sems):
    head = NODE_BLK
    parts = qkv_ref.shape[0]
    jobs = [(qkv_ref, w_ref.at[pl.ds(0, parts)])]
    jobs += [
        (out_ref.at[:, pl.ds(k * head, head)], w_ref.at[parts, pl.ds(k * head, head)])
        for k in range(HEADS)
    ]
    copies = [pltpu.make_async_copy(a, b, sems.at[k]) for k, (a, b) in enumerate(jobs)]
    for c in copies:
        c.start()
    for c in copies:
        c.wait()


def packed(qkv, out_w):
    parts, width, head = qkv.shape
    return pl.pallas_call(
        pack_kernel,
        in_specs=[HBM] * 2,
        out_specs=VMEM,
        out_shape=in_vmem((parts + 1, width, head)),
        scratch_shapes=[pltpu.SemaphoreType.DMA((1 + HEADS,))],
        name="pack_weights",
        compiler_params=pltpu.CompilerParams(vmem_limit_bytes=4 * MIB),
    )(kept_in_hbm(qkv), kept_in_hbm(out_w))


def write_kv(x_ref, wkv_ref, kv_ref, first):
    rows, width = x_ref.shape
    for r in range(0, rows, ROWS):
        out = bf(matmul(x_ref[r : r + ROWS], wkv_ref[...]))
        at = first + r // NODE_BLK
        kv_ref[at : at + ROWS // NODE_BLK] = out.reshape((ROWS // NODE_BLK, NODE_BLK, 2 * width))


def kv_first_kernel(xa, xb, w0, w1, w2, w3, kv_ref, q_ref, wkv_ref, wo_ref, wq_ref):
    head = NODE_BLK
    share = my_place()[1]
    for h, w in enumerate((w0, w1, w2, w3)):
        at = (h // 2) * 4 * head + (h % 2) * head
        wq_ref[:, h * head : (h + 1) * head] = w[0]
        wkv_ref[:, at : at + head] = w[1]
        wkv_ref[:, at + 2 * head : at + 3 * head] = w[2]
        for k in range(HEADS):
            block = slice(k * head, (k + 1) * head)
            wo_ref[h * head : (h + 1) * head, block] = w[3, block]
    write_kv(xa, wkv_ref, kv_ref, 0)
    write_kv(xb, wkv_ref, kv_ref, xa.shape[0] // NODE_BLK)
    q_ref[...] = bf(matmul(xa[aligned(share, q_ref.shape[0])], wq_ref[...]))


def kv_first(xa, xb, weights, slots):
    rows, width = xa.shape
    return pl.pallas_call(
        kv_first_kernel,
        in_specs=[VMEM] * (2 + len(weights)),
        out_specs=[VMEM] * 4,
        scratch_shapes=[pltpu.VMEM((width, width), jnp.bfloat16)],
        out_shape=[
            in_vmem((slots * rows // NODE_BLK, NODE_BLK, 2 * width)),
            in_vmem((rows // 2, width)),
            in_vmem((width, 2 * width)),
            in_vmem((width, width)),
        ],
        name="kv_first",
        compiler_params=pltpu.CompilerParams(vmem_limit_bytes=12 * MIB),
    )(xa, xb, *weights)


def kv_second_kernel(xa, xb, wkv_ref, kv_in, kv_ref):
    first = 2 * xa.shape[0] // NODE_BLK
    write_kv(xa, wkv_ref, kv_ref, first)
    write_kv(xb, wkv_ref, kv_ref, first + xa.shape[0] // NODE_BLK)


def kv_second(xa, xb, wkv, kv):
    rows, width = xa.shape
    return pl.pallas_call(
        kv_second_kernel,
        in_specs=[VMEM] * 4,
        out_specs=VMEM,
        out_shape=in_vmem(kv.shape),
        input_output_aliases={3: 0},
        name="kv_second",
        compiler_params=pltpu.CompilerParams(vmem_limit_bytes=12 * MIB),
    )(xa, xb, wkv, kv)


def attend_kernel(
    list_ref, count_ref, relay_ref, q_ref, wkv_ref, kv_in, heads_ref, kv, *, doms, per_dev
):
    _, share, par, _, dom = my_place()
    head = NODE_BLK
    rows, width = q_ref.shape
    write_kv(relay_ref, wkv_ref, kv, 4 * per_dev)

    scale = math.log2(math.e) / math.sqrt(head)
    blocks = rows // NODE_BLK
    for b in range(blocks):
        row = share * blocks + b
        count = count_ref[row]
        where = []
        for j in range(KMAX):
            entry = list_ref[row, j]
            part = lax.div(entry, per_dev)
            step = lax.rem(part - dom + (doms + 2), doms) - 2
            turned = jnp.where(par == 0, step, -step)
            slot = jnp.where(turned >= 0, turned, turned + 5)
            where.append(slot * per_dev + lax.rem(entry, per_dev))
        at = slice(b * NODE_BLK, (b + 1) * NODE_BLK)
        for pair in range(HEADS // 2):
            col = pair * 4 * head
            keys = jnp.concatenate([kv[i, :, col : col + 2 * head] for i in where], axis=0)
            vals = jnp.concatenate(
                [kv[i, :, col + 2 * head : col + 4 * head] for i in where], axis=0
            )
            q0 = q_ref[at, 2 * pair * head : (2 * pair + 1) * head]
            q1 = q_ref[at, (2 * pair + 1) * head : (2 * pair + 2) * head]
            zero = jnp.zeros_like(q0)
            query = jnp.concatenate(
                [jnp.concatenate([q0, zero], axis=1), jnp.concatenate([zero, q1], axis=1)], axis=0
            )
            scores = lax.dot_general(
                query, keys, (((1,), (1,)), ((), ())), preferred_element_type=jnp.float32
            )
            parts = [
                jnp.where(j < count, scores[:, j * NODE_BLK : (j + 1) * NODE_BLK], -1e30)
                for j in range(KMAX)
            ]
            top = jnp.max(functools.reduce(jnp.maximum, parts), axis=-1, keepdims=True)
            parts = [jnp.exp2((p - top) * scale) for p in parts]
            total = jnp.sum(functools.reduce(jnp.add, parts), axis=-1, keepdims=True)
            mixed = matmul(jnp.concatenate([bf(p) for p in parts], axis=1), vals) / total
            heads_ref[at, 2 * pair * head : (2 * pair + 1) * head] = bf(mixed[:head, :head])
            heads_ref[at, (2 * pair + 1) * head : (2 * pair + 2) * head] = bf(mixed[head:, head:])


def attend(listed, counts, relay, query, wkv, kv, per_dev, doms):
    rows, width = query.shape
    return pl.pallas_call(
        functools.partial(attend_kernel, doms=doms, per_dev=per_dev),
        in_specs=[SMEM] * 2 + [VMEM] * 4,
        out_specs=[VMEM] * 2,
        out_shape=[in_vmem((rows, width)), in_vmem(kv.shape)],
        input_output_aliases={5: 1},
        name="attend",
        compiler_params=pltpu.CompilerParams(vmem_limit_bytes=12 * MIB),
    )(listed, counts, relay, query, wkv, kv)[0]


def silu(v):
    return 0.5 * v * (1.0 + jnp.tanh(0.5 * v))


def mlp_first_kernel(
    heads_ref, gain_ref, shift_ref, wo_ref, u0, d0, u1, d1, u2, d2, state_ref,
    resid_ref, normed_ref,
    rows_in, hidden_ref, sem,
):
    sample, share, _, _, _ = my_place()
    rows, width = heads_ref.shape
    copy = pltpu.make_async_copy(state_ref.at[sample, aligned(share, rows)], rows_in, sem)
    copy.start()
    mixed = matmul(heads_ref[...], wo_ref[...])
    copy.wait()
    resid_ref[...] = rows_in[...].astype(jnp.float32) + mixed
    s = pl.ds(sample, 1)
    normed_ref[...] = bf(normalise(resid_ref[...], gain_ref[1, s], shift_ref[1, s]))
    for k, u in enumerate((u0, u1, u2)):
        hidden_ref[:, k * width : (k + 1) * width] = bf(silu(matmul(normed_ref[...], u[...])))
    downs = jnp.concatenate([d0[...], d1[...], d2[...]], axis=0)
    resid_ref[...] += matmul(hidden_ref[...], downs)


def mlp_first(heads, gain, shift, wo, weights, state):
    rows, width = heads.shape
    return pl.pallas_call(
        mlp_first_kernel,
        in_specs=[VMEM] * (4 + len(weights)) + [HBM],
        out_specs=[VMEM] * 2,
        out_shape=[in_vmem((rows, width), jnp.float32), in_vmem((rows, width))],
        scratch_shapes=[
            pltpu.VMEM((rows, width), jnp.bfloat16),
            pltpu.VMEM((rows, 3 * width), jnp.bfloat16),
            pltpu.SemaphoreType.DMA,
        ],
        name="mlp_first",
        compiler_params=pltpu.CompilerParams(vmem_limit_bytes=12 * MIB),
    )(heads, gain, shift, wo, *weights, kept_in_hbm(state))


def mlp_second_kernel(resid_ref, normed_ref, u_ref, d_ref, o0, o1, o2, o3, total_ref):
    rank = my_place()[3]
    head = NODE_BLK
    hidden = bf(silu(matmul(normed_ref[...], u_ref[...])))
    total_ref[...] = resid_ref[...] + matmul(hidden, d_ref[...])
    for r, o_ref in enumerate((o0, o1, o2, o3)):
        o_ref[...] = bf(total_ref[:, aligned(lax.rem(rank + r, HEADS), head)])


def mlp_second(resid, normed, u, d):
    rows, width = normed.shape
    return pl.pallas_call(
        mlp_second_kernel,
        in_specs=[VMEM] * 4,
        out_specs=[VMEM] * HEADS,
        out_shape=[in_vmem((rows, width // HEADS))] * HEADS,
        scratch_shapes=[pltpu.VMEM((rows, width), jnp.float32)],
        name="mlp_second",
        compiler_params=pltpu.CompilerParams(vmem_limit_bytes=12 * MIB),
    )(resid, normed, u, d)


def place_kernel(own, across, after, before, o_ref):
    rank = my_place()[3]
    for off, r in ((0, own), (2, across), (1, after), (3, before)):
        o_ref[lax.rem(rank + off, HEADS)] = r[...]


def placed_rows(pieces):
    rows, head = pieces[0].shape
    return pl.pallas_call(
        place_kernel,
        in_specs=[VMEM] * HEADS,
        out_specs=VMEM,
        out_shape=shape((HEADS, rows, head)),
        name="place_rows",
        compiler_params=pltpu.CompilerParams(vmem_limit_bytes=4 * MIB),
    )(*pieces)


def after(value, *deps):
    return lax.optimization_barrier((value, *deps))[0]


def local(
    state, norm_gain, norm_shift, qkv_weight, out_weight, up_weight, down_weight, neighbours, counts
):
    samples, row_count, width = state.shape
    per_dev = row_count // NODE_BLK
    doms = lax.axis_size("dom")
    tps = lax.axis_size("tp")
    def hop(v, pairs):
        return lax.ppermute(v, "dom", pairs)

    def sign(i):
        return 1 if i % 2 == 0 else -1

    def swap(v):
        return hop(v, [(i ^ 1, i) for i in range(doms)])

    def near(v):
        return hop(v, [((i + 2 * sign(i)) % doms, i) for i in range(doms)])

    def far(v):
        return hop(v, [((i - 2 * sign(i)) % doms, i) for i in range(doms)])

    def ring(v):
        pairs = [
            (i * tps + (t - sign(i)) % tps, i * tps + t) for i in range(doms) for t in range(tps)
        ]
        return lax.ppermute(v, ("dom", "tp"), pairs)

    def up(v):
        return lax.ppermute(v, "tp", [(i, (i + 1) % tps) for i in range(tps)])

    def down(v):
        return lax.ppermute(v, "tp", [((i + 1) % tps, i) for i in range(tps)])

    def across(v):
        return lax.ppermute(v, "tp", [(i, (i + 2) % tps) for i in range(tps)])

    own = normed_rows(state, norm_gain, norm_shift)
    partner = swap(own)
    near_rows, far_rows = near(own), far(own)

    qkv, own = lax.optimization_barrier((qkv_weight, own))
    w0 = packed(jnp.transpose(qkv, (1, 0, 2)), out_weight)

    def gather(own_w, own_up):
        first = ring(own_w)
        return first, swap(first), ring(first), ring(own_up)

    def never(own_w, own_up):
        return own_w, own_w, own_w, own_up

    w1, w2, w3, u1 = lax.cond(lax.axis_index("tp") >= 0, gather, never, w0, up_weight)
    d1 = ring(after(down_weight, w1))

    kv, query, wkv, wo = kv_first(own, partner, (w0, w1, w2, w3), 5)
    u1, query = lax.optimization_barrier((u1, query))
    u3 = ring(u1)
    near_rows, far_rows, query = lax.optimization_barrier((near_rows, far_rows, query))
    relay = swap(near_rows)
    kv = kv_second(near_rows, far_rows, wkv, kv)
    u1, d1, kv = lax.optimization_barrier((u1, d1, kv))
    u2, d2, d3 = swap(u1), swap(d1), ring(d1)

    heads = attend(neighbours, counts, relay, query, wkv, kv, per_dev, doms)
    weights = (up_weight, down_weight, u1, d1, u2, d2)
    resid, normed = mlp_first(heads, norm_gain, norm_shift, wo, weights, state)
    mine = mlp_second(resid, normed, u3, d3)
    out = placed_rows((mine[0], across(mine[2]), down(mine[3]), up(mine[1])))
    return out.reshape(samples, row_count, width // tps)


def solution(mesh):
    placed = (
        P(None, "dom", None),
        P(),
        P(),
        P(None, None, "tp"),
        P("tp", None),
        P(None, "tp"),
        P("tp", None),
        P("dom", None),
        P("dom"),
    )
    return jax.shard_map(
        local, mesh=mesh, in_specs=placed, out_specs=P(None, "dom", "tp"), check_vma=False
    )
```

```python
import functools
import math

import jax
import jax.numpy as jnp
from jax import lax
from jax.experimental import pallas as pl
from jax.experimental.pallas import tpu as pltpu
from jax.sharding import PartitionSpec as P

HEADS = 4
NODE_BLK = 128
KMAX = 8
ROWS = 512
MIB = 1024 * 1024

VMEM = pl.BlockSpec(memory_space=pltpu.VMEM)
SMEM = pl.BlockSpec(memory_space=pltpu.SMEM)
HBM = pl.BlockSpec(memory_space=pltpu.HBM)


def bf(v):
    return v.astype(jnp.bfloat16)


def matmul(a, b):
    return jnp.dot(a, b, preferred_element_type=jnp.float32)


def aligned(i, step):
    return pl.ds(pl.multiple_of(i * step, step), step)


def shape(dims, dtype=jnp.bfloat16):
    return jax.ShapeDtypeStruct(dims, dtype)


def in_hbm(dims, dtype=jnp.bfloat16):
    return pltpu.HBM(dims, dtype)


def in_vmem(dims, dtype=jnp.bfloat16):
    return pltpu.VMEM(dims, dtype)


def kept_in_hbm(v):
    return pltpu.with_memory_space_constraint(v, pltpu.HBM)


def normalise(values, gain, shift):
    mean = jnp.mean(values, axis=-1, keepdims=True)
    centred = values - mean
    spread = jnp.mean(centred * centred, axis=-1, keepdims=True)
    return centred * lax.rsqrt(spread + 1e-05) * gain + shift


def my_place():
    dom = lax.axis_index("dom")
    rank = lax.axis_index("tp")
    return lax.div(rank, 2), lax.rem(rank, 2), lax.rem(dom, 2), rank, dom


def prepare_kernel(
    state_ref, gain_ref, shift_ref, qkv_ref, out_ref, o_ref, w_ref, x_in, out_in, affine, sems
):
    sample = my_place()[0]
    s = pl.ds(sample, 1)
    head = NODE_BLK
    chunks = 4
    step = x_in.shape[0] // chunks
    parts = qkv_ref.shape[0]
    spans = [pl.ds(k * step, step) for k in range(chunks)]
    jobs = [(state_ref.at[sample, at], x_in.at[at]) for at in spans]
    jobs += [(gain_ref, affine.at[0]), (shift_ref, affine.at[1])]
    jobs += [(qkv_ref, w_ref.at[pl.ds(0, parts)]), (out_ref, out_in)]
    copies = [pltpu.make_async_copy(a, b, sems.at[k]) for k, (a, b) in enumerate(jobs)]
    for k in (0, chunks, chunks + 1, *range(1, chunks), *range(chunks + 2, len(jobs))):
        copies[k].start()
    for c in copies[chunks : chunks + 2]:
        c.wait()
    gain, shift = affine[0, 0, s], affine[1, 0, s]
    for c, at in zip(copies, spans):
        c.wait()
        o_ref[at] = bf(normalise(x_in[at].astype(jnp.float32), gain, shift))
    for c in copies[chunks + 2 :]:
        c.wait()
    for k in range(HEADS):
        block = slice(k * head, (k + 1) * head)
        w_ref[parts, block] = out_in[:, block]


def prepare(state, gain, shift, qkv, out_w):
    _, rows, width = state.shape
    parts, _, head = qkv.shape
    return pl.pallas_call(
        prepare_kernel,
        in_specs=[HBM] * 5,
        out_specs=[VMEM] * 2,
        out_shape=[in_vmem((rows, width)), in_vmem((parts + 1, width, head))],
        scratch_shapes=[
            pltpu.VMEM((rows, width), jnp.bfloat16),
            pltpu.VMEM(out_w.shape, jnp.bfloat16),
            pltpu.VMEM((2, *gain.shape), jnp.float32),
            pltpu.SemaphoreType.DMA((8,)),
        ],
        name="prepare",
        compiler_params=pltpu.CompilerParams(vmem_limit_bytes=6 * MIB),
    )(*[kept_in_hbm(v) for v in (state, gain, shift, qkv, out_w)])


def relay_kernel(a_ref, b_ref, o_ref):
    par = my_place()[2]

    @pl.when(par == 0)
    def _():
        o_ref[...] = a_ref[...]

    @pl.when(par == 1)
    def _():
        o_ref[...] = b_ref[...]


def one_to_relay(a, b):
    return pl.pallas_call(
        relay_kernel,
        in_specs=[VMEM] * 2,
        out_specs=VMEM,
        out_shape=in_vmem(a.shape),
        name="one_to_relay",
        compiler_params=pltpu.CompilerParams(vmem_limit_bytes=4 * MIB),
    )(a, b)


def write_kv(x_ref, wkv_ref, kv_ref, first):
    rows, width = x_ref.shape
    for r in range(0, rows, ROWS):
        out = bf(matmul(x_ref[r : r + ROWS], wkv_ref[...]))
        at = first + r // NODE_BLK
        kv_ref[at : at + ROWS // NODE_BLK] = out.reshape((ROWS // NODE_BLK, NODE_BLK, 2 * width))


def kv_first_kernel(xa, xb, w0, w1, w2, w3m, w3t, kv_ref, q_ref, wkv_ref, wo_ref, wq_ref):
    head = NODE_BLK
    _, share, par, _, _ = my_place()
    half = w3m.shape[1]
    halves = ((par, w3m), (1 - par, w3t))
    for h in range(HEADS):
        at = (h // 2) * 4 * head + (h % 2) * head
        spots = ((0, wq_ref, h * head), (1, wkv_ref, at), (2, wkv_ref, at + 2 * head))
        for c, dst, col in spots:
            if h < 3:
                dst[:, col : col + head] = (w0, w1, w2)[h][c]
            else:
                for which, w in halves:
                    dst[aligned(which, half), col : col + head] = w[c]
        rows = slice(h * head, (h + 1) * head)
        if h < 3:
            for k in range(HEADS):
                wo_ref[rows, k * head : (k + 1) * head] = (w0, w1, w2)[h][3, k * head : (k + 1) * head]
        else:
            for which, w in halves:
                for k in range(HEADS // 2):
                    wo_ref[rows, aligned(which * (HEADS // 2) + k, head)] = w[
                        3, k * head : (k + 1) * head
                    ]
    write_kv(xa, wkv_ref, kv_ref, 0)
    write_kv(xb, wkv_ref, kv_ref, xa.shape[0] // NODE_BLK)
    q_ref[...] = bf(matmul(xa[aligned(share, q_ref.shape[0])], wq_ref[...]))


def kv_first(xa, xb, weights, slots):
    rows, width = xa.shape
    return pl.pallas_call(
        kv_first_kernel,
        in_specs=[VMEM] * (2 + len(weights)),
        out_specs=[VMEM] * 4,
        scratch_shapes=[pltpu.VMEM((width, width), jnp.bfloat16)],
        out_shape=[
            in_vmem((slots * rows // NODE_BLK, NODE_BLK, 2 * width)),
            in_vmem((rows // 2, width)),
            in_vmem((width, 2 * width)),
            in_vmem((width, width)),
        ],
        name="kv_first",
        compiler_params=pltpu.CompilerParams(vmem_limit_bytes=12 * MIB),
    )(xa, xb, *weights)


def kv_second_kernel(xa, xb, wkv_ref, kv_in, kv_ref):
    first = 2 * xa.shape[0] // NODE_BLK
    write_kv(xa, wkv_ref, kv_ref, first)
    write_kv(xb, wkv_ref, kv_ref, first + xa.shape[0] // NODE_BLK)


def kv_second(xa, xb, wkv, kv):
    rows, width = xa.shape
    return pl.pallas_call(
        kv_second_kernel,
        in_specs=[VMEM] * 4,
        out_specs=VMEM,
        out_shape=in_vmem(kv.shape),
        input_output_aliases={3: 0},
        name="kv_second",
        compiler_params=pltpu.CompilerParams(vmem_limit_bytes=12 * MIB),
    )(xa, xb, wkv, kv)


def attend_kernel(
    list_ref, count_ref, relay_ref, q_ref, wkv_ref, kv_in, heads_ref, kv, *, doms, per_dev
):
    _, share, par, _, dom = my_place()
    head = NODE_BLK
    rows, width = q_ref.shape
    write_kv(relay_ref, wkv_ref, kv, 4 * per_dev)

    scale = math.log2(math.e) / math.sqrt(head)
    blocks = rows // NODE_BLK
    for b in range(blocks):
        row = share * blocks + b
        count = count_ref[row]
        where = []
        for j in range(KMAX):
            entry = list_ref[row, j]
            part = lax.div(entry, per_dev)
            step = lax.rem(part - dom + (doms + 2), doms) - 2
            turned = jnp.where(par == 0, step, -step)
            close = jnp.where(turned < 0, 4, turned)
            slot = jnp.where(step == 2, 2, jnp.where(step == -2, 3, close))
            where.append(slot * per_dev + lax.rem(entry, per_dev))
        at = slice(b * NODE_BLK, (b + 1) * NODE_BLK)
        for pair in range(HEADS // 2):
            col = pair * 4 * head
            keys = jnp.concatenate([kv[i, :, col : col + 2 * head] for i in where], axis=0)
            vals = jnp.concatenate(
                [kv[i, :, col + 2 * head : col + 4 * head] for i in where], axis=0
            )
            q0 = q_ref[at, 2 * pair * head : (2 * pair + 1) * head]
            q1 = q_ref[at, (2 * pair + 1) * head : (2 * pair + 2) * head]
            zero = jnp.zeros_like(q0)
            query = jnp.concatenate(
                [jnp.concatenate([q0, zero], axis=1), jnp.concatenate([zero, q1], axis=1)], axis=0
            )
            scores = lax.dot_general(
                query, keys, (((1,), (1,)), ((), ())), preferred_element_type=jnp.float32
            )
            parts = [
                jnp.where(j < count, scores[:, j * NODE_BLK : (j + 1) * NODE_BLK], -1e30)
                for j in range(KMAX)
            ]
            top = jnp.max(functools.reduce(jnp.maximum, parts), axis=-1, keepdims=True)
            parts = [jnp.exp2((p - top) * scale) for p in parts]
            total = jnp.sum(functools.reduce(jnp.add, parts), axis=-1, keepdims=True)
            mixed = matmul(jnp.concatenate([bf(p) for p in parts], axis=1), vals) / total
            heads_ref[at, 2 * pair * head : (2 * pair + 1) * head] = bf(mixed[:head, :head])
            heads_ref[at, (2 * pair + 1) * head : (2 * pair + 2) * head] = bf(mixed[head:, head:])


def attend(listed, counts, relay, query, wkv, kv, per_dev, doms):
    rows, width = query.shape
    return pl.pallas_call(
        functools.partial(attend_kernel, doms=doms, per_dev=per_dev),
        in_specs=[SMEM] * 2 + [VMEM] * 4,
        out_specs=[VMEM] * 2,
        out_shape=[in_vmem((rows, width)), in_vmem(kv.shape)],
        input_output_aliases={5: 1},
        name="attend",
        compiler_params=pltpu.CompilerParams(vmem_limit_bytes=12 * MIB),
    )(listed, counts, relay, query, wkv, kv)[0]


def silu(v):
    return 0.5 * v * (1.0 + jnp.tanh(0.5 * v))


def mlp_first_kernel(
    heads_ref, gain_ref, shift_ref, wo_ref, u0, d0, u1, d1, u2, d2, state_ref,
    resid_ref, normed_ref,
    rows_in, hidden_ref, sem,
):
    sample, share, _, _, _ = my_place()
    rows, width = heads_ref.shape
    copy = pltpu.make_async_copy(state_ref.at[sample, aligned(share, rows)], rows_in, sem)
    copy.start()
    mixed = matmul(heads_ref[...], wo_ref[...])
    copy.wait()
    resid_ref[...] = rows_in[...].astype(jnp.float32) + mixed
    s = pl.ds(sample, 1)
    normed_ref[...] = bf(normalise(resid_ref[...], gain_ref[1, s], shift_ref[1, s]))
    for k, u in enumerate((u0, u1, u2)):
        hidden_ref[:, k * width : (k + 1) * width] = bf(silu(matmul(normed_ref[...], u[...])))
    downs = jnp.concatenate([d0[...], d1[...], d2[...]], axis=0)
    resid_ref[...] += matmul(hidden_ref[...], downs)


def mlp_first(heads, gain, shift, wo, weights, state):
    rows, width = heads.shape
    return pl.pallas_call(
        mlp_first_kernel,
        in_specs=[VMEM] * (4 + len(weights)) + [HBM],
        out_specs=[VMEM] * 2,
        out_shape=[in_vmem((rows, width), jnp.float32), in_vmem((rows, width))],
        scratch_shapes=[
            pltpu.VMEM((rows, width), jnp.bfloat16),
            pltpu.VMEM((rows, 3 * width), jnp.bfloat16),
            pltpu.SemaphoreType.DMA,
        ],
        name="mlp_first",
        compiler_params=pltpu.CompilerParams(vmem_limit_bytes=12 * MIB),
    )(heads, gain, shift, wo, *weights, kept_in_hbm(state))


def mlp_second_kernel(resid_ref, normed_ref, mine, theirs, o0, o1, o2, o3, total_ref, up_ref, down_ref):
    _, _, par, rank, _ = my_place()
    head = NODE_BLK

    @pl.when(par == 0)
    def _():
        up_ref[...] = mine[...]
        down_ref[...] = theirs[...]

    @pl.when(par == 1)
    def _():
        up_ref[...] = theirs[...]
        down_ref[...] = mine[...]

    hidden = bf(silu(matmul(normed_ref[...], up_ref[...])))
    total_ref[...] = resid_ref[...] + matmul(hidden, down_ref[...])
    for r, o_ref in enumerate((o0, o1, o2, o3)):
        o_ref[...] = bf(total_ref[:, aligned(lax.rem(rank + r, HEADS), head)])


def mlp_second(resid, normed, mine, theirs):
    rows, width = normed.shape
    return pl.pallas_call(
        mlp_second_kernel,
        in_specs=[VMEM] * 4,
        out_specs=[VMEM] * HEADS,
        out_shape=[in_vmem((rows, width // HEADS))] * HEADS,
        scratch_shapes=[
            pltpu.VMEM((rows, width), jnp.float32),
            pltpu.VMEM(mine.shape, jnp.bfloat16),
            pltpu.VMEM(mine.shape, jnp.bfloat16),
        ],
        name="mlp_second",
        compiler_params=pltpu.CompilerParams(vmem_limit_bytes=12 * MIB),
    )(resid, normed, mine, theirs)


def place_kernel(own, across, after, before, o_ref):
    rank = my_place()[3]
    for off, r in ((0, own), (2, across), (1, after), (3, before)):
        o_ref[lax.rem(rank + off, HEADS)] = r[...]


def placed_rows(pieces):
    rows, head = pieces[0].shape
    return pl.pallas_call(
        place_kernel,
        in_specs=[VMEM] * HEADS,
        out_specs=VMEM,
        out_shape=shape((HEADS, rows, head)),
        name="place_rows",
        compiler_params=pltpu.CompilerParams(vmem_limit_bytes=4 * MIB),
    )(*pieces)


def after(value, *deps):
    return lax.optimization_barrier((value, *deps))[0]


def local(
    state, norm_gain, norm_shift, qkv_weight, out_weight, up_weight, down_weight, neighbours, counts
):
    samples, row_count, width = state.shape
    per_dev = row_count // NODE_BLK
    doms = lax.axis_size("dom")
    tps = lax.axis_size("tp")
    dom = lax.axis_index("dom")
    par = lax.rem(dom, 2)

    def hop(v, pairs):
        return lax.ppermute(v, "dom", pairs)

    def sign(i):
        return 1 if i % 2 == 0 else -1

    def swap(v):
        return hop(v, [(i ^ 1, i) for i in range(doms)])

    def shifted(v, by):
        return hop(v, [(i, (i + by) % doms) for i in range(doms)])

    def ring(v):
        pairs = [
            (i * tps + (t - sign(i)) % tps, i * tps + t) for i in range(doms) for t in range(tps)
        ]
        return lax.ppermute(v, ("dom", "tp"), pairs)

    def up(v):
        return lax.ppermute(v, "tp", [(i, (i + 1) % tps) for i in range(tps)])

    def down(v):
        return lax.ppermute(v, "tp", [((i + 1) % tps, i) for i in range(tps)])

    def across(v):
        return lax.ppermute(v, "tp", [(i, (i + 2) % tps) for i in range(tps)])

    qkv = jnp.transpose(qkv_weight, (1, 0, 2))
    own, w0 = prepare(state, norm_gain, norm_shift, qkv, out_weight)
    w1 = ring(w0)
    partner = swap(own)
    before, beyond = shifted(own, 2), shifted(own, -2)
    u1 = ring(after(up_weight, own))

    w1 = after(w1, partner)
    w2 = swap(w1)
    mid = width // 2
    w1_half = lax.dynamic_slice_in_dim(w1, par * mid, mid, 1)
    w3m = ring(w1_half)
    w3t = swap(w3m)
    d1 = ring(after(down_weight, w3t))

    own_late, u1 = lax.optimization_barrier((own, u1))
    kv, query, wkv, wo = kv_first(own_late, partner, (w0, w1, w2, w3m, w3t), 5)
    before, beyond, query = lax.optimization_barrier((before, beyond, query))
    relay = swap(one_to_relay(beyond, before))
    kv = kv_second(beyond, before, wkv, kv)
    u2, d2 = swap(u1), swap(d1)
    relayed, kv = lax.optimization_barrier((one_to_relay(u1, d1), kv))
    last = ring(relayed)

    heads = attend(neighbours, counts, relay, query, wkv, kv, per_dev, doms)
    last, heads = lax.optimization_barrier((last, heads))
    last_too = swap(last)
    weights = (up_weight, down_weight, u1, d1, u2, d2)
    resid, normed = mlp_first(heads, norm_gain, norm_shift, wo, weights, state)
    mine = mlp_second(resid, normed, last, last_too)
    out = placed_rows((mine[0], across(mine[2]), down(mine[3]), up(mine[1])))
    return out.reshape(samples, row_count, width // tps)


def solution(mesh):
    placed = (
        P(None, "dom", None),
        P(),
        P(),
        P(None, None, "tp"),
        P("tp", None),
        P(None, "tp"),
        P("tp", None),
        P("dom", None),
        P("dom"),
    )
    return jax.shard_map(
        local, mesh=mesh, in_specs=placed, out_specs=P(None, "dom", "tp"), check_vma=False
    )
```

```python
import functools
import math

import jax
import jax.numpy as jnp
from jax import lax
from jax.experimental import pallas as pl
from jax.experimental.pallas import tpu as pltpu
from jax.sharding import PartitionSpec as P

HEADS = 4
NODE_BLK = 128
KMAX = 8
ROWS = 512
MIB = 1024 * 1024

VMEM = pl.BlockSpec(memory_space=pltpu.VMEM)
SMEM = pl.BlockSpec(memory_space=pltpu.SMEM)
HBM = pl.BlockSpec(memory_space=pltpu.HBM)


def bf(v):
    return v.astype(jnp.bfloat16)


def matmul(a, b):
    return jnp.dot(a, b, preferred_element_type=jnp.float32)


def aligned(i, step):
    return pl.ds(pl.multiple_of(i * step, step), step)


def shape(dims, dtype=jnp.bfloat16):
    return jax.ShapeDtypeStruct(dims, dtype)


def in_hbm(dims, dtype=jnp.bfloat16):
    return pltpu.HBM(dims, dtype)


def in_vmem(dims, dtype=jnp.bfloat16):
    return pltpu.VMEM(dims, dtype)


def kept_in_hbm(v):
    return pltpu.with_memory_space_constraint(v, pltpu.HBM)


def normalise(values, gain, shift):
    mean = jnp.mean(values, axis=-1, keepdims=True)
    centred = values - mean
    spread = jnp.mean(centred * centred, axis=-1, keepdims=True)
    return centred * lax.rsqrt(spread + 1e-05) * gain + shift


def my_place():
    dom = lax.axis_index("dom")
    rank = lax.axis_index("tp")
    return lax.div(rank, 2), lax.rem(rank, 2), lax.rem(dom, 2), rank, dom


def prepare_kernel(
    state_ref, gain_ref, shift_ref, qkv_ref, out_ref, o_ref, w_ref, x_in, out_in, affine, sems
):
    sample = my_place()[0]
    s = pl.ds(sample, 1)
    head = NODE_BLK
    chunks = 4
    step = x_in.shape[0] // chunks
    parts = qkv_ref.shape[0]
    spans = [pl.ds(k * step, step) for k in range(chunks)]
    jobs = [(state_ref.at[sample, at], x_in.at[at]) for at in spans]
    jobs += [(gain_ref, affine.at[0]), (shift_ref, affine.at[1])]
    jobs += [(qkv_ref, w_ref.at[pl.ds(0, parts)]), (out_ref, out_in)]
    copies = [pltpu.make_async_copy(a, b, sems.at[k]) for k, (a, b) in enumerate(jobs)]
    for k in (0, chunks, chunks + 1, *range(1, chunks), *range(chunks + 2, len(jobs))):
        copies[k].start()
    for c in copies[chunks : chunks + 2]:
        c.wait()
    gain, shift = affine[0, 0, s], affine[1, 0, s]
    for c, at in zip(copies, spans):
        c.wait()
        o_ref[at] = bf(normalise(x_in[at].astype(jnp.float32), gain, shift))
    for c in copies[chunks + 2 :]:
        c.wait()
    for k in range(HEADS):
        block = slice(k * head, (k + 1) * head)
        w_ref[parts, block] = out_in[:, block]


def prepare(state, gain, shift, qkv, out_w):
    _, rows, width = state.shape
    parts, _, head = qkv.shape
    return pl.pallas_call(
        prepare_kernel,
        in_specs=[HBM] * 5,
        out_specs=[VMEM] * 2,
        out_shape=[in_vmem((rows, width)), in_vmem((parts + 1, width, head))],
        scratch_shapes=[
            pltpu.VMEM((rows, width), jnp.bfloat16),
            pltpu.VMEM(out_w.shape, jnp.bfloat16),
            pltpu.VMEM((2, *gain.shape), jnp.float32),
            pltpu.SemaphoreType.DMA((8,)),
        ],
        name="prepare",
        compiler_params=pltpu.CompilerParams(vmem_limit_bytes=6 * MIB),
    )(*[kept_in_hbm(v) for v in (state, gain, shift, qkv, out_w)])


def write_kv(x_ref, wkv_ref, kv_ref, first):
    rows, width = x_ref.shape
    for r in range(0, rows, ROWS):
        out = bf(matmul(x_ref[r : r + ROWS], wkv_ref[...]))
        at = first + r // NODE_BLK
        kv_ref[at : at + ROWS // NODE_BLK] = out.reshape((ROWS // NODE_BLK, NODE_BLK, 2 * width))


def kv_first_kernel(xa, xb, w0, w1, w2, w3, kv_ref, q_ref, wkv_ref, wo_ref, wq_ref):
    head = NODE_BLK
    share = my_place()[1]
    for h, w in enumerate((w0, w1, w2, w3)):
        at = (h // 2) * 4 * head + (h % 2) * head
        wq_ref[:, h * head : (h + 1) * head] = w[0]
        wkv_ref[:, at : at + head] = w[1]
        wkv_ref[:, at + 2 * head : at + 3 * head] = w[2]
        for k in range(HEADS):
            block = slice(k * head, (k + 1) * head)
            wo_ref[h * head : (h + 1) * head, block] = w[3, block]
    write_kv(xa, wkv_ref, kv_ref, 0)
    write_kv(xb, wkv_ref, kv_ref, xa.shape[0] // NODE_BLK)
    q_ref[...] = bf(matmul(xa[aligned(share, q_ref.shape[0])], wq_ref[...]))


def kv_first(xa, xb, weights, slots):
    rows, width = xa.shape
    return pl.pallas_call(
        kv_first_kernel,
        in_specs=[VMEM] * (2 + len(weights)),
        out_specs=[VMEM] * 4,
        scratch_shapes=[pltpu.VMEM((width, width), jnp.bfloat16)],
        out_shape=[
            in_vmem((slots * rows // NODE_BLK, NODE_BLK, 2 * width)),
            in_vmem((rows // 2, width)),
            in_vmem((width, 2 * width)),
            in_vmem((width, width)),
        ],
        name="kv_first",
        compiler_params=pltpu.CompilerParams(vmem_limit_bytes=12 * MIB),
    )(xa, xb, *weights)


def kv_second_kernel(xa, xb, wkv_ref, kv_in, kv_ref):
    first = 2 * xa.shape[0] // NODE_BLK
    write_kv(xa, wkv_ref, kv_ref, first)
    write_kv(xb, wkv_ref, kv_ref, first + xa.shape[0] // NODE_BLK)


def kv_second(xa, xb, wkv, kv):
    rows, width = xa.shape
    return pl.pallas_call(
        kv_second_kernel,
        in_specs=[VMEM] * 4,
        out_specs=VMEM,
        out_shape=in_vmem(kv.shape),
        input_output_aliases={3: 0},
        name="kv_second",
        compiler_params=pltpu.CompilerParams(vmem_limit_bytes=12 * MIB),
    )(xa, xb, wkv, kv)


def attend_kernel(
    list_ref, count_ref, relay_ref, q_ref, wkv_ref, kv_in, heads_ref, kv, *, doms, per_dev
):
    _, share, par, _, dom = my_place()
    head = NODE_BLK
    rows, width = q_ref.shape
    write_kv(relay_ref, wkv_ref, kv, 4 * per_dev)

    scale = math.log2(math.e) / math.sqrt(head)
    blocks = rows // NODE_BLK
    for b in range(blocks):
        row = share * blocks + b
        count = count_ref[row]
        where = []
        for j in range(KMAX):
            entry = list_ref[row, j]
            part = lax.div(entry, per_dev)
            step = lax.rem(part - dom + (doms + 2), doms) - 2
            turned = jnp.where(par == 0, step, -step)
            slot = jnp.where(turned >= 0, turned, turned + 5)
            where.append(slot * per_dev + lax.rem(entry, per_dev))
        at = slice(b * NODE_BLK, (b + 1) * NODE_BLK)
        for pair in range(HEADS // 2):
            col = pair * 4 * head
            keys = jnp.concatenate([kv[i, :, col : col + 2 * head] for i in where], axis=0)
            vals = jnp.concatenate(
                [kv[i, :, col + 2 * head : col + 4 * head] for i in where], axis=0
            )
            q0 = q_ref[at, 2 * pair * head : (2 * pair + 1) * head]
            q1 = q_ref[at, (2 * pair + 1) * head : (2 * pair + 2) * head]
            zero = jnp.zeros_like(q0)
            query = jnp.concatenate(
                [jnp.concatenate([q0, zero], axis=1), jnp.concatenate([zero, q1], axis=1)], axis=0
            )
            scores = lax.dot_general(
                query, keys, (((1,), (1,)), ((), ())), preferred_element_type=jnp.float32
            )
            parts = [
                jnp.where(j < count, scores[:, j * NODE_BLK : (j + 1) * NODE_BLK], -1e30)
                for j in range(KMAX)
            ]
            top = jnp.max(functools.reduce(jnp.maximum, parts), axis=-1, keepdims=True)
            parts = [jnp.exp2((p - top) * scale) for p in parts]
            total = jnp.sum(functools.reduce(jnp.add, parts), axis=-1, keepdims=True)
            mixed = matmul(jnp.concatenate([bf(p) for p in parts], axis=1), vals) / total
            heads_ref[at, 2 * pair * head : (2 * pair + 1) * head] = bf(mixed[:head, :head])
            heads_ref[at, (2 * pair + 1) * head : (2 * pair + 2) * head] = bf(mixed[head:, head:])


def attend(listed, counts, relay, query, wkv, kv, per_dev, doms):
    rows, width = query.shape
    return pl.pallas_call(
        functools.partial(attend_kernel, doms=doms, per_dev=per_dev),
        in_specs=[SMEM] * 2 + [VMEM] * 4,
        out_specs=[VMEM] * 2,
        out_shape=[in_vmem((rows, width)), in_vmem(kv.shape)],
        input_output_aliases={5: 1},
        name="attend",
        compiler_params=pltpu.CompilerParams(vmem_limit_bytes=12 * MIB),
    )(listed, counts, relay, query, wkv, kv)[0]


def silu(v):
    return 0.5 * v * (1.0 + jnp.tanh(0.5 * v))


def mlp_kernel(
    heads_ref, gain_ref, shift_ref, wo_ref, u0, d0, u1, d1, u2, d2, u3, d3, state_ref,
    o0, o1, o2, o3,
    resid_ref, normed_ref, rows_in, hidden_ref, sem,
):
    sample, share, _, rank, _ = my_place()
    head = NODE_BLK
    rows, width = heads_ref.shape
    copy = pltpu.make_async_copy(state_ref.at[sample, aligned(share, rows)], rows_in, sem)
    copy.start()
    mixed = matmul(heads_ref[...], wo_ref[...])
    copy.wait()
    resid_ref[...] = rows_in[...].astype(jnp.float32) + mixed
    s = pl.ds(sample, 1)
    normed_ref[...] = bf(normalise(resid_ref[...], gain_ref[1, s], shift_ref[1, s]))
    for k, u in enumerate((u0, u1, u2, u3)):
        hidden_ref[:, k * width : (k + 1) * width] = bf(silu(matmul(normed_ref[...], u[...])))
    downs = jnp.concatenate([d0[...], d1[...], d2[...], d3[...]], axis=0)
    resid_ref[...] += matmul(hidden_ref[...], downs)
    for r, o_ref in enumerate((o0, o1, o2, o3)):
        o_ref[...] = bf(resid_ref[:, aligned(lax.rem(rank + r, HEADS), head)])


def mlp(heads, gain, shift, wo, weights, state):
    rows, width = heads.shape
    return pl.pallas_call(
        mlp_kernel,
        in_specs=[VMEM] * (4 + len(weights)) + [HBM],
        out_specs=[VMEM] * HEADS,
        out_shape=[in_vmem((rows, width // HEADS))] * HEADS,
        scratch_shapes=[
            pltpu.VMEM((rows, width), jnp.float32),
            pltpu.VMEM((rows, width), jnp.bfloat16),
            pltpu.VMEM((rows, width), jnp.bfloat16),
            pltpu.VMEM((rows, HEADS * width), jnp.bfloat16),
            pltpu.SemaphoreType.DMA,
        ],
        name="mlp",
        compiler_params=pltpu.CompilerParams(vmem_limit_bytes=14 * MIB),
    )(heads, gain, shift, wo, *weights, kept_in_hbm(state))


def place_kernel(own, across, after, before, o_ref):
    rank = my_place()[3]
    for off, r in ((0, own), (2, across), (1, after), (3, before)):
        o_ref[lax.rem(rank + off, HEADS)] = r[...]


def placed_rows(pieces):
    rows, head = pieces[0].shape
    return pl.pallas_call(
        place_kernel,
        in_specs=[VMEM] * HEADS,
        out_specs=VMEM,
        out_shape=shape((HEADS, rows, head)),
        name="place_rows",
        compiler_params=pltpu.CompilerParams(vmem_limit_bytes=4 * MIB),
    )(*pieces)


def after(value, *deps):
    return lax.optimization_barrier((value, *deps))[0]


def local(
    state, norm_gain, norm_shift, qkv_weight, out_weight, up_weight, down_weight, neighbours, counts
):
    samples, row_count, width = state.shape
    per_dev = row_count // NODE_BLK
    doms = lax.axis_size("dom")
    tps = lax.axis_size("tp")

    def hop(v, pairs):
        return lax.ppermute(v, "dom", pairs)

    def sign(i):
        return 1 if i % 2 == 0 else -1

    def swap(v):
        return hop(v, [(i ^ 1, i) for i in range(doms)])

    def near(v):
        return hop(v, [((i + 2 * sign(i)) % doms, i) for i in range(doms)])

    def far(v):
        return hop(v, [((i - 2 * sign(i)) % doms, i) for i in range(doms)])

    def ring(v):
        pairs = [
            (i * tps + (t - sign(i)) % tps, i * tps + t) for i in range(doms) for t in range(tps)
        ]
        return lax.ppermute(v, ("dom", "tp"), pairs)

    def up(v):
        return lax.ppermute(v, "tp", [(i, (i + 1) % tps) for i in range(tps)])

    def down(v):
        return lax.ppermute(v, "tp", [((i + 1) % tps, i) for i in range(tps)])

    def across(v):
        return lax.ppermute(v, "tp", [(i, (i + 2) % tps) for i in range(tps)])

    qkv = jnp.transpose(qkv_weight, (1, 0, 2))
    own, w0 = prepare(state, norm_gain, norm_shift, qkv, out_weight)
    w1 = ring(w0)
    partner = swap(own)
    near_rows, far_rows = near(own), far(own)
    u1 = ring(after(up_weight, own))

    w1 = after(w1, partner)
    w2, w3 = swap(w1), ring(w1)
    d1 = ring(after(down_weight, w1))

    own_late, u1 = lax.optimization_barrier((own, u1))
    kv, query, wkv, wo = kv_first(own_late, partner, (w0, w1, w2, w3), 5)
    u3, d3 = ring(u1), ring(d1)
    near_rows, far_rows, query, u1, d1 = lax.optimization_barrier(
        (near_rows, far_rows, query, u1, d1)
    )
    relay = swap(near_rows)
    kv = kv_second(near_rows, far_rows, wkv, kv)
    u2, d2 = swap(u1), swap(d1)

    heads = attend(neighbours, counts, relay, query, wkv, kv, per_dev, doms)
    weights = (up_weight, down_weight, u1, d1, u2, d2, u3, d3)
    mine = mlp(heads, norm_gain, norm_shift, wo, weights, state)
    out = placed_rows((mine[0], across(mine[2]), down(mine[3]), up(mine[1])))
    return out.reshape(samples, row_count, width // tps)


def solution(mesh):
    placed = (
        P(None, "dom", None),
        P(),
        P(),
        P(None, None, "tp"),
        P("tp", None),
        P(None, "tp"),
        P("tp", None),
        P("dom", None),
        P("dom"),
    )
    return jax.shard_map(
        local, mesh=mesh, in_specs=placed, out_specs=P(None, "dom", "tp"), check_vma=False
    )
```

```python
import functools
import math

import jax
import jax.numpy as jnp
from jax import lax
from jax.experimental import pallas as pl
from jax.experimental.pallas import tpu as pltpu
from jax.sharding import PartitionSpec as P

HEADS = 4
NODE_BLK = 128
KMAX = 8
ROWS = 512
MIB = 1024 * 1024

VMEM = pl.BlockSpec(memory_space=pltpu.VMEM)
SMEM = pl.BlockSpec(memory_space=pltpu.SMEM)
HBM = pl.BlockSpec(memory_space=pltpu.HBM)


def bf(v):
    return v.astype(jnp.bfloat16)


def matmul(a, b):
    return jnp.dot(a, b, preferred_element_type=jnp.float32)


def aligned(i, step):
    return pl.ds(pl.multiple_of(i * step, step), step)


def shape(dims, dtype=jnp.bfloat16):
    return jax.ShapeDtypeStruct(dims, dtype)


def in_hbm(dims, dtype=jnp.bfloat16):
    return pltpu.HBM(dims, dtype)


def in_vmem(dims, dtype=jnp.bfloat16):
    return pltpu.VMEM(dims, dtype)


def kept_in_hbm(v):
    return pltpu.with_memory_space_constraint(v, pltpu.HBM)


def normalise(values, gain, shift):
    mean = jnp.mean(values, axis=-1, keepdims=True)
    centred = values - mean
    spread = jnp.mean(centred * centred, axis=-1, keepdims=True)
    return centred * lax.rsqrt(spread + 1e-05) * gain + shift


def my_place():
    dom = lax.axis_index("dom")
    rank = lax.axis_index("tp")
    return lax.div(rank, 2), lax.rem(rank, 2), lax.rem(dom, 2), rank, dom


def prepare_kernel(
    state_ref, gain_ref, shift_ref, qkv_ref, out_ref, o_ref, w_ref, x_in, affine, sems
):
    sample = my_place()[0]
    s = pl.ds(sample, 1)
    head = NODE_BLK
    chunks = 4
    step = x_in.shape[0] // chunks
    parts = qkv_ref.shape[0]
    spans = [pl.ds(k * step, step) for k in range(chunks)]
    jobs = [(state_ref.at[sample, at], x_in.at[at]) for at in spans]
    jobs += [(gain_ref, affine.at[0]), (shift_ref, affine.at[1]), (qkv_ref, w_ref.at[pl.ds(0, parts)])]
    jobs += [
        (out_ref.at[:, pl.ds(k * head, head)], w_ref.at[parts, pl.ds(k * head, head)])
        for k in range(HEADS)
    ]
    copies = [pltpu.make_async_copy(a, b, sems.at[k]) for k, (a, b) in enumerate(jobs)]
    for k in (0, chunks, chunks + 1, *range(1, chunks), *range(chunks + 2, len(jobs))):
        copies[k].start()
    for c in copies[chunks : chunks + 2]:
        c.wait()
    gain, shift = affine[0, 0, s], affine[1, 0, s]
    for c, at in zip(copies, spans):
        c.wait()
        o_ref[at] = bf(normalise(x_in[at].astype(jnp.float32), gain, shift))
    for c in copies[chunks + 2 :]:
        c.wait()


def prepare(state, gain, shift, qkv, out_w):
    _, rows, width = state.shape
    parts, _, head = qkv.shape
    return pl.pallas_call(
        prepare_kernel,
        in_specs=[HBM] * 5,
        out_specs=[VMEM] * 2,
        out_shape=[in_vmem((rows, width)), in_vmem((parts + 1, width, head))],
        scratch_shapes=[
            pltpu.VMEM((rows, width), jnp.bfloat16),
            pltpu.VMEM((2, *gain.shape), jnp.float32),
            pltpu.SemaphoreType.DMA((7 + HEADS,)),
        ],
        name="prepare",
        compiler_params=pltpu.CompilerParams(vmem_limit_bytes=6 * MIB),
    )(*[kept_in_hbm(v) for v in (state, gain, shift, qkv, out_w)])


def relay_kernel(a_ref, b_ref, o_ref):
    par = my_place()[2]

    @pl.when(par == 0)
    def _():
        o_ref[...] = a_ref[...]

    @pl.when(par == 1)
    def _():
        o_ref[...] = b_ref[...]


def one_to_relay(a, b):
    return pl.pallas_call(
        relay_kernel,
        in_specs=[VMEM] * 2,
        out_specs=VMEM,
        out_shape=in_vmem(a.shape),
        name="one_to_relay",
        compiler_params=pltpu.CompilerParams(vmem_limit_bytes=4 * MIB),
    )(a, b)


def write_kv(x_ref, wkv_ref, kv_ref, first):
    rows, width = x_ref.shape
    for r in range(0, rows, ROWS):
        out = bf(matmul(x_ref[r : r + ROWS], wkv_ref[...]))
        at = first + r // NODE_BLK
        kv_ref[at : at + ROWS // NODE_BLK] = out.reshape((ROWS // NODE_BLK, NODE_BLK, 2 * width))


def kv_first_kernel(xa, xb, w0, w1, w2, w3m, w3t, kv_ref, q_ref, wkv_ref, wo_ref, wq_ref):
    head = NODE_BLK
    _, share, par, _, _ = my_place()
    half = w3m.shape[1]
    halves = ((par, w3m), (1 - par, w3t))
    for h in range(HEADS):
        at = (h // 2) * 4 * head + (h % 2) * head
        spots = ((0, wq_ref, h * head), (1, wkv_ref, at), (2, wkv_ref, at + 2 * head))
        for c, dst, col in spots:
            if h < 3:
                dst[:, col : col + head] = (w0, w1, w2)[h][c]
            else:
                for which, w in halves:
                    dst[aligned(which, half), col : col + head] = w[c]
        rows = slice(h * head, (h + 1) * head)
        if h < 3:
            for k in range(HEADS):
                wo_ref[rows, k * head : (k + 1) * head] = (w0, w1, w2)[h][3, k * head : (k + 1) * head]
        else:
            for which, w in halves:
                for k in range(HEADS // 2):
                    wo_ref[rows, aligned(which * (HEADS // 2) + k, head)] = w[
                        3, k * head : (k + 1) * head
                    ]
    write_kv(xa, wkv_ref, kv_ref, 0)
    write_kv(xb, wkv_ref, kv_ref, xa.shape[0] // NODE_BLK)
    q_ref[...] = bf(matmul(xa[aligned(share, q_ref.shape[0])], wq_ref[...]))


def kv_first(xa, xb, weights, slots):
    rows, width = xa.shape
    return pl.pallas_call(
        kv_first_kernel,
        in_specs=[VMEM] * (2 + len(weights)),
        out_specs=[VMEM] * 4,
        scratch_shapes=[pltpu.VMEM((width, width), jnp.bfloat16)],
        out_shape=[
            in_vmem((slots * rows // NODE_BLK, NODE_BLK, 2 * width)),
            in_vmem((rows // 2, width)),
            in_vmem((width, 2 * width)),
            in_vmem((width, width)),
        ],
        name="kv_first",
        compiler_params=pltpu.CompilerParams(vmem_limit_bytes=12 * MIB),
    )(xa, xb, *weights)


def kv_second_kernel(xa, xb, wkv_ref, kv_in, kv_ref):
    first = 2 * xa.shape[0] // NODE_BLK
    write_kv(xa, wkv_ref, kv_ref, first)
    write_kv(xb, wkv_ref, kv_ref, first + xa.shape[0] // NODE_BLK)


def kv_second(xa, xb, wkv, kv):
    rows, width = xa.shape
    return pl.pallas_call(
        kv_second_kernel,
        in_specs=[VMEM] * 4,
        out_specs=VMEM,
        out_shape=in_vmem(kv.shape),
        input_output_aliases={3: 0},
        name="kv_second",
        compiler_params=pltpu.CompilerParams(vmem_limit_bytes=12 * MIB),
    )(xa, xb, wkv, kv)


def attend_kernel(
    list_ref, count_ref, relay_ref, q_ref, wkv_ref, kv_in, heads_ref, kv, *, doms, per_dev
):
    _, share, par, _, dom = my_place()
    head = NODE_BLK
    rows, width = q_ref.shape
    write_kv(relay_ref, wkv_ref, kv, 4 * per_dev)

    scale = math.log2(math.e) / math.sqrt(head)
    blocks = rows // NODE_BLK
    for b in range(blocks):
        row = share * blocks + b
        count = count_ref[row]
        where = []
        for j in range(KMAX):
            entry = list_ref[row, j]
            part = lax.div(entry, per_dev)
            step = lax.rem(part - dom + (doms + 2), doms) - 2
            turned = jnp.where(par == 0, step, -step)
            slot = jnp.where(turned >= 0, turned, turned + 5)
            where.append(slot * per_dev + lax.rem(entry, per_dev))
        at = slice(b * NODE_BLK, (b + 1) * NODE_BLK)
        for pair in range(HEADS // 2):
            col = pair * 4 * head
            keys = jnp.concatenate([kv[i, :, col : col + 2 * head] for i in where], axis=0)
            vals = jnp.concatenate(
                [kv[i, :, col + 2 * head : col + 4 * head] for i in where], axis=0
            )
            q0 = q_ref[at, 2 * pair * head : (2 * pair + 1) * head]
            q1 = q_ref[at, (2 * pair + 1) * head : (2 * pair + 2) * head]
            zero = jnp.zeros_like(q0)
            query = jnp.concatenate(
                [jnp.concatenate([q0, zero], axis=1), jnp.concatenate([zero, q1], axis=1)], axis=0
            )
            scores = lax.dot_general(
                query, keys, (((1,), (1,)), ((), ())), preferred_element_type=jnp.float32
            )
            parts = [
                jnp.where(j < count, scores[:, j * NODE_BLK : (j + 1) * NODE_BLK], -1e30)
                for j in range(KMAX)
            ]
            top = jnp.max(functools.reduce(jnp.maximum, parts), axis=-1, keepdims=True)
            parts = [jnp.exp2((p - top) * scale) for p in parts]
            total = jnp.sum(functools.reduce(jnp.add, parts), axis=-1, keepdims=True)
            mixed = matmul(jnp.concatenate([bf(p) for p in parts], axis=1), vals) / total
            heads_ref[at, 2 * pair * head : (2 * pair + 1) * head] = bf(mixed[:head, :head])
            heads_ref[at, (2 * pair + 1) * head : (2 * pair + 2) * head] = bf(mixed[head:, head:])


def attend(listed, counts, relay, query, wkv, kv, per_dev, doms):
    rows, width = query.shape
    return pl.pallas_call(
        functools.partial(attend_kernel, doms=doms, per_dev=per_dev),
        in_specs=[SMEM] * 2 + [VMEM] * 4,
        out_specs=[VMEM] * 2,
        out_shape=[in_vmem((rows, width)), in_vmem(kv.shape)],
        input_output_aliases={5: 1},
        name="attend",
        compiler_params=pltpu.CompilerParams(vmem_limit_bytes=12 * MIB),
    )(listed, counts, relay, query, wkv, kv)[0]


def silu(v):
    return 0.5 * v * (1.0 + jnp.tanh(0.5 * v))


def mlp_first_kernel(
    heads_ref, gain_ref, shift_ref, wo_ref, u0, d0, u1, d1, u2, d2, state_ref,
    resid_ref, normed_ref,
    rows_in, hidden_ref, sem,
):
    sample, share, _, _, _ = my_place()
    rows, width = heads_ref.shape
    copy = pltpu.make_async_copy(state_ref.at[sample, aligned(share, rows)], rows_in, sem)
    copy.start()
    mixed = matmul(heads_ref[...], wo_ref[...])
    copy.wait()
    resid_ref[...] = rows_in[...].astype(jnp.float32) + mixed
    s = pl.ds(sample, 1)
    normed_ref[...] = bf(normalise(resid_ref[...], gain_ref[1, s], shift_ref[1, s]))
    for k, u in enumerate((u0, u1, u2)):
        hidden_ref[:, k * width : (k + 1) * width] = bf(silu(matmul(normed_ref[...], u[...])))
    downs = jnp.concatenate([d0[...], d1[...], d2[...]], axis=0)
    resid_ref[...] += matmul(hidden_ref[...], downs)


def mlp_first(heads, gain, shift, wo, weights, state):
    rows, width = heads.shape
    return pl.pallas_call(
        mlp_first_kernel,
        in_specs=[VMEM] * (4 + len(weights)) + [HBM],
        out_specs=[VMEM] * 2,
        out_shape=[in_vmem((rows, width), jnp.float32), in_vmem((rows, width))],
        scratch_shapes=[
            pltpu.VMEM((rows, width), jnp.bfloat16),
            pltpu.VMEM((rows, 3 * width), jnp.bfloat16),
            pltpu.SemaphoreType.DMA,
        ],
        name="mlp_first",
        compiler_params=pltpu.CompilerParams(vmem_limit_bytes=12 * MIB),
    )(heads, gain, shift, wo, *weights, kept_in_hbm(state))


def mlp_second_kernel(resid_ref, normed_ref, mine, theirs, o0, o1, o2, o3, total_ref, up_ref, down_ref):
    _, _, par, rank, _ = my_place()
    head = NODE_BLK

    @pl.when(par == 0)
    def _():
        up_ref[...] = mine[...]
        down_ref[...] = theirs[...]

    @pl.when(par == 1)
    def _():
        up_ref[...] = theirs[...]
        down_ref[...] = mine[...]

    hidden = bf(silu(matmul(normed_ref[...], up_ref[...])))
    total_ref[...] = resid_ref[...] + matmul(hidden, down_ref[...])
    for r, o_ref in enumerate((o0, o1, o2, o3)):
        o_ref[...] = bf(total_ref[:, aligned(lax.rem(rank + r, HEADS), head)])


def mlp_second(resid, normed, mine, theirs):
    rows, width = normed.shape
    return pl.pallas_call(
        mlp_second_kernel,
        in_specs=[VMEM] * 4,
        out_specs=[VMEM] * HEADS,
        out_shape=[in_vmem((rows, width // HEADS))] * HEADS,
        scratch_shapes=[
            pltpu.VMEM((rows, width), jnp.float32),
            pltpu.VMEM(mine.shape, jnp.bfloat16),
            pltpu.VMEM(mine.shape, jnp.bfloat16),
        ],
        name="mlp_second",
        compiler_params=pltpu.CompilerParams(vmem_limit_bytes=12 * MIB),
    )(resid, normed, mine, theirs)


def place_kernel(own, across, after, before, o_ref):
    rank = my_place()[3]
    for off, r in ((0, own), (2, across), (1, after), (3, before)):
        o_ref[lax.rem(rank + off, HEADS)] = r[...]


def placed_rows(pieces):
    rows, head = pieces[0].shape
    return pl.pallas_call(
        place_kernel,
        in_specs=[VMEM] * HEADS,
        out_specs=VMEM,
        out_shape=shape((HEADS, rows, head)),
        name="place_rows",
        compiler_params=pltpu.CompilerParams(vmem_limit_bytes=4 * MIB),
    )(*pieces)


def after(value, *deps):
    return lax.optimization_barrier((value, *deps))[0]


def local(
    state, norm_gain, norm_shift, qkv_weight, out_weight, up_weight, down_weight, neighbours, counts
):
    samples, row_count, width = state.shape
    per_dev = row_count // NODE_BLK
    doms = lax.axis_size("dom")
    tps = lax.axis_size("tp")
    dom = lax.axis_index("dom")
    par = lax.rem(dom, 2)

    def hop(v, pairs):
        return lax.ppermute(v, "dom", pairs)

    def sign(i):
        return 1 if i % 2 == 0 else -1

    def swap(v):
        return hop(v, [(i ^ 1, i) for i in range(doms)])

    def near(v):
        return hop(v, [((i + 2 * sign(i)) % doms, i) for i in range(doms)])

    def far(v):
        return hop(v, [((i - 2 * sign(i)) % doms, i) for i in range(doms)])

    def ring(v):
        pairs = [
            (i * tps + (t - sign(i)) % tps, i * tps + t) for i in range(doms) for t in range(tps)
        ]
        return lax.ppermute(v, ("dom", "tp"), pairs)

    def up(v):
        return lax.ppermute(v, "tp", [(i, (i + 1) % tps) for i in range(tps)])

    def down(v):
        return lax.ppermute(v, "tp", [((i + 1) % tps, i) for i in range(tps)])

    def across(v):
        first = [
            (i * tps + t, i * tps + (t + 2 if i % 2 == 0 else t - 1) % tps)
            for i in range(doms)
            for t in range(tps)
        ]
        then = [
            (i * tps + t, i * tps + (t if i % 2 == 0 else t - 1) % tps)
            for i in range(doms)
            for t in range(tps)
        ]
        return lax.ppermute(lax.ppermute(v, ("dom", "tp"), first), ("dom", "tp"), then)

    qkv = jnp.transpose(qkv_weight, (1, 0, 2))
    own, w0 = prepare(state, norm_gain, norm_shift, qkv, out_weight)
    w1 = ring(w0)
    partner = swap(own)
    near_rows, far_rows = near(own), far(own)
    u1 = ring(after(up_weight, own))

    w1 = after(w1, partner)
    w2 = swap(w1)
    mid = width // 2
    w1_half = lax.dynamic_slice_in_dim(w1, par * mid, mid, 1)
    w3m = ring(w1_half)
    w3t = swap(w3m)
    d1 = ring(after(down_weight, w3m))

    own_late, u1 = lax.optimization_barrier((own, u1))
    kv, query, wkv, wo = kv_first(own_late, partner, (w0, w1, w2, w3m, w3t), 5)
    relayed = one_to_relay(u1, d1)
    near_rows, far_rows, query, relayed = lax.optimization_barrier(
        (near_rows, far_rows, query, relayed)
    )
    last = ring(relayed)
    relay = swap(near_rows)
    kv = kv_second(near_rows, far_rows, wkv, kv)
    u2, d2 = swap(u1), swap(d1)

    heads = attend(neighbours, counts, relay, query, wkv, kv, per_dev, doms)
    last, heads = lax.optimization_barrier((last, heads))
    last_too = swap(last)
    weights = (up_weight, down_weight, u1, d1, u2, d2)
    resid, normed = mlp_first(heads, norm_gain, norm_shift, wo, weights, state)
    mine = mlp_second(resid, normed, last, last_too)
    out = placed_rows((mine[0], across(mine[2]), down(mine[3]), up(mine[1])))
    return out.reshape(samples, row_count, width // tps)


def solution(mesh):
    placed = (
        P(None, "dom", None),
        P(),
        P(),
        P(None, None, "tp"),
        P("tp", None),
        P(None, "tp"),
        P("tp", None),
        P("dom", None),
        P("dom"),
    )
    return jax.shard_map(
        local, mesh=mesh, in_specs=placed, out_specs=P(None, "dom", "tp"), check_vma=False
    )
```
